256 devices in a mesh: rows: 32 (over z, y), blk: 8 (over x, core).
Axes of the slice: x: 4, y: 4, z: 8, core: 2. Of those that a mesh axis runs over, the one named last changes fastest.
Arguments:
- acol: int32 [512, 32], P('rows', 'blk'), may hold values from -1 to 511, as said below
- aval: bfloat16 [512, 32, 128, 128], P('rows', 'blk'), may hold values from -0.109375 to 0.109375
- mcol: int32 [2, 512, 4], P(None, 'rows'), may hold values from 0 to 255, as said below
- mval: bfloat16 [2, 512, 4, 128, 128], P(None, 'rows'), may hold values from -12 to 12
- rpat: int32 [2, 512, 2], P(None, 'rows'), may hold values from 0 to 255, as said below
- scol: int32 [2, 256], replicated, may hold values from 0 to 511, as said below
- cand: int32 [2, 512, 2], P(None, 'rows'), may hold values from 0 to 255, as said below
Outputs:
- resid: bfloat16 [2, 512, 2, 128, 128], P(None, 'rows', None, None, 'blk')
- scores: float32 [2, 512, 2, 128], P(None, 'rows', None, 'blk')
The draws below stay inside these ranges and needn't reach their ends.
Inputs may be any that keep to these rules, and one draw needn't show every extreme that they name: `acol`: each block row lists 27 different block columns, each at most 16 block rows from the row itself, counted cyclically modulo 512; its other 5 entries are -1. `mcol`: the entries of one block row in one slab differ. `rpat`: the entries of one block row in one slab differ. `scol`: the entries of one slab differ. `cand`: the entries of one block row in one slab differ.
All inputs are finite; a program needn't handle non-finite values.
Results may differ from the reference program's by a relative error of at most 0.0025.
Values may be sent and summed in bfloat16 or wider, within the bound.
A program may use at most 128 MiB of HBM per device.

```python
import jax
import jax.numpy as jnp
from jax import lax

BS = 128
KA = 27
KS = 32
SLABS = 2
QM = 4
Q = 2
C = 2
RB_DEV = 16
NB = 512
SC = 256


slab_reach = 6


def pick_near(key, lead_shape, wanted, half_span, centers, modulus):
    options = 2 * half_span + 1
    ranking = jax.random.randint(key, lead_shape + (options,), 0, 1 << 20) * options + jnp.arange(options, dtype=jnp.int32)
    chosen = jnp.argsort(ranking, axis=-1)[..., :wanted].astype(jnp.int32)
    return ((centers[..., None] + chosen - half_span) % modulus).astype(jnp.int32)


def draw_acol(key, part):
    centers = jnp.arange(NB, dtype=jnp.int32)
    chosen = pick_near(jax.random.fold_in(key, 11), (NB,), KA, RB_DEV, centers, NB)
    slot_rank = jnp.argsort(jax.random.randint(jax.random.fold_in(key, 12), (NB, KS), 0, 1 << 20) * KS + jnp.arange(KS, dtype=jnp.int32), axis=1)
    filled = jnp.full((NB, KS), -1, dtype=jnp.int32)
    filled = filled.at[jnp.arange(NB)[:, None], slot_rank[:, :KA]].set(chosen)
    return filled.astype(jnp.int32)


def slab_centers():
    return jnp.broadcast_to(jnp.arange(NB, dtype=jnp.int32) // 2, (SLABS, NB))


def draw_mcol(key, part):
    return pick_near(jax.random.fold_in(key, 21), (SLABS, NB), QM, slab_reach, slab_centers(), SC)


def draw_rpat(key, part):
    return pick_near(jax.random.fold_in(key, 31), (SLABS, NB), Q, slab_reach, slab_centers(), SC)


def draw_cand(key, part):
    return pick_near(jax.random.fold_in(key, 41), (SLABS, NB), C, slab_reach, slab_centers(), SC)


def draw_scol(key, part):
    jitter = jax.random.randint(jax.random.fold_in(key, 51), (SLABS, SC), 0, 2)
    return (2 * jnp.arange(SC, dtype=jnp.int32)[None, :] + jitter).astype(jnp.int32)


def levels(rng, shape, shards, low, largest):
    gain, own = 1.0, jax.random.fold_in(rng, 6)
    for axis_at, parts in shards:
        steps = jnp.exp(jax.random.uniform(jax.random.fold_in(own, axis_at), (parts,), jnp.float32, low / len(shards), largest / len(shards)))
        gain = gain * jnp.repeat(steps, shape[axis_at] // parts).reshape([-1 if axis == axis_at else 1 for axis in range(len(shape))])
    return gain


def gaussian(own_key, dims, spread, bound, split=(), kind=jnp.bfloat16):
    values = spread * jax.random.normal(own_key, dims, jnp.float32)
    if split:
        values = values * levels(own_key, dims, split, -0.22, 0.18)
    return jnp.clip(values, -bound, bound).astype(kind)


def setup_inputs(seed: int = 0) -> dict:
    seeds = jax.random.split(jax.random.key(seed), 8)
    return {
        "acol": draw_acol(jax.random.fold_in(seeds[7], 71), 0),
        "aval": gaussian(seeds[1], (NB, KS, BS, BS), (KA * BS) ** -0.5, 0.109375, ((0, 32), (1, 8))),
        "mcol": draw_mcol(jax.random.fold_in(seeds[7], 71), 0),
        "mval": gaussian(seeds[3], (SLABS, NB, QM, BS, BS), 2.0, 12.0, ((1, 32),)),
        "rpat": draw_rpat(jax.random.fold_in(seeds[7], 71), 0),
        "scol": draw_scol(jax.random.fold_in(seeds[7], 71), 0),
        "cand": draw_cand(jax.random.fold_in(seeds[7], 71), 0),
    }


def reference(acol, aval, mcol, mval, rpat, scol, cand):
    total_rows = acol.shape[0]
    block_size = aval.shape[2]
    identity = jnp.eye(block_size, dtype=jnp.float32)
    slab_range = jnp.arange(scol.shape[1], dtype=jnp.int32)
    resid_list = []
    score_list = []
    for slab_idx in range(SLABS):
        m_values = mval[slab_idx]
        m_columns = mcol[slab_idx]
        pattern_all = rpat[slab_idx]
        slab_owner = scol[slab_idx]
        cand_all = cand[slab_idx]

        def residual_row(row_id):
            columns = acol[row_id]
            present = columns >= 0
            safe_cols = jnp.where(present, columns, 0).astype(jnp.int32)
            blocks = aval[row_id].astype(jnp.float32)
            m_near = m_values[safe_cols].astype(jnp.float32)
            products = jnp.einsum('sab,sqbc->sqac', blocks, m_near)
            pattern = pattern_all[row_id]
            matches = ((m_columns[safe_cols][:, :, None] == pattern[None, None, :]) & present[:, None, None]).astype(jnp.float32)
            summed = jnp.einsum('sqp,sqac->pac', matches, products)
            owners = jnp.sum(jnp.where(pattern[:, None] == slab_range[None, :], slab_owner[None, :], 0), axis=1)
            on_diag = (owners == row_id).astype(jnp.float32)
            return (summed - on_diag[:, None, None] * identity).astype(jnp.bfloat16)

        resid_slab = lax.map(residual_row, jnp.arange(total_rows, dtype=jnp.int32))

        def score_row(row_id):
            columns = acol[row_id]
            present = columns >= 0
            safe_cols = jnp.where(present, columns, 0).astype(jnp.int32)
            blocks = aval[row_id].astype(jnp.float32)
            r_near = resid_slab[safe_cols].astype(jnp.float32)
            patterns = pattern_all[safe_cols]
            matches = ((patterns[:, :, None] == cand_all[row_id][None, None, :]) & present[:, None, None]).astype(jnp.float32)
            chosen = jnp.einsum('sqc,sqab->scab', matches, r_near)
            projected = jnp.einsum('sxy,scyz->cxz', blocks, chosen)
            return jnp.mean(projected * projected, axis=1)

        score_slab = lax.map(score_row, jnp.arange(total_rows, dtype=jnp.int32))
        resid_list.append(resid_slab)
        score_list.append(score_slab)
    return jnp.stack(resid_list), jnp.stack(score_list)
```

```python
import functools

import jax
import jax.numpy as jnp
from jax import lax
from jax.experimental import pallas as pl
from jax.experimental.pallas import tpu as pltpu
from jax.sharding import PartitionSpec as P

MESH = pl.DeviceIdType.MESH
CORES = 2


def kernel(
    dims,
    scol_s, cand_s, rpat_s, acol_h, mcol_h, rpat_h, aval_h, mval_h,
    o_res, o_sc,
    a_win, m_win, r_win, r_turn, sc_own, ac_v, mc_v, rp_v,
    ac_s, mc_s, rp_s, idx_m, idx_r, diag,
    a_send, a_recv, m_send, m_recv, r_send, r_recv,
    ac_send, ac_recv, mc_send, mc_recv, rp_send, rp_recv,
    o_send, o_recv, s_send, s_recv, loc,
):
    rings, blks, rows, own, per, qm, q2, n = dims
    chips = blks // CORES
    reach = rows
    total = rings * rows
    r, b = lax.axis_index("rows"), lax.axis_index("blk")
    x, t = b // CORES, b % CORES
    up, down = lax.rem(r + 1, rings), lax.rem(r + rings - 1, rings)
    mate = (r, CORES * x + (1 - t))
    mq, rq = own * qm, own * q2
    zero_m, zero_r = m_win.shape[0] - 1, r_win.shape[0] - 1

    def remote(src, dst, send, recv, where):
        return pltpu.make_async_remote_copy(
            src_ref=src, dst_ref=dst, send_sem=send, recv_sem=recv,
            device_id=where, device_id_type=MESH,
        )

    def across(d):
        return lax.rem(x + d, chips)

    def chip(d):
        return CORES * across(d) + t

    home_a = pltpu.make_async_copy(aval_h.at[pl.ds(own * x, own)], a_win.at[b], loc.at[0])
    home_a.start()
    home_m = pltpu.make_async_copy(
        mval_h.at[t], m_win.at[pl.ds(mq * (chips - x), mq * chips)], loc.at[1]
    )
    home_m.start()
    home_ac = pltpu.make_async_copy(acol_h, ac_v.at[b], loc.at[2])
    home_mc = pltpu.make_async_copy(mcol_h.at[t], mc_v.at[1], loc.at[3])
    home_rp = pltpu.make_async_copy(rpat_h.at[t], rp_v.at[1], loc.at[4])
    for copy in (home_ac, home_mc, home_rp):
        copy.start()

    barrier = pltpu.get_barrier_semaphore()
    for d in range(1, blks):
        pl.semaphore_signal(
            barrier, inc=1, device_id=(r, lax.rem(b + d, blks)), device_id_type=MESH
        )
    for ring in (up, down):
        for d in range(chips):
            pl.semaphore_signal(barrier, inc=1, device_id=(ring, chip(d)), device_id_type=MESH)
    m_win[zero_m] = jnp.zeros((n, n), m_win.dtype)
    r_win[zero_r] = jnp.zeros((n, n), r_win.dtype)
    pl.semaphore_wait(barrier, blks - 1 + 2 * chips)

    ints = []
    for d in range(1, blks):
        to = lax.rem(b + d, blks)
        ints.append(remote(acol_h, ac_v.at[b], ac_send.at[d], ac_recv.at[b], (r, to)))
    for k, ring in ((0, up), (2, down)):
        ints.append(remote(mcol_h.at[t], mc_v.at[k], mc_send.at[k], mc_recv.at[k], (ring, b)))
        ints.append(remote(rpat_h.at[t], rp_v.at[k], rp_send.at[k], rp_recv.at[k], (ring, b)))
    for copy in ints:
        copy.start()

    m_out = []
    for j in range(chips):
        src = mval_h.at[t, pl.ds(mq * j, mq)]
        for cond, slot, ring, k in (
            (x <= j, j - x, up, 0),
            (x >= j, 2 * chips + j - x, down, 1),
        ):
            safe = jnp.clip(slot, 0, 2 * chips)
            m_out.append((cond, remote(
                src, m_win.at[pl.ds(mq * safe, mq)], m_send.at[chips * k + j], m_recv.at[safe],
                (ring, b),
            )))
    a_out = {}
    for d in (1, chips - 1) + tuple(range(2, chips - 1)):
        a_out[d] = remote(
            aval_h.at[pl.ds(own * across(d), own)], a_win.at[b],
            a_send.at[d], a_recv.at[b], (r, chip(d)),
        )
        a_out[d].start()
    for cond, copy in m_out:
        pl.when(cond)(copy.start)
    home_a.wait()
    swaps = [remote(a_win.at[b], a_win.at[b], a_send.at[chips], a_recv.at[b], mate)]
    swaps[0].start()

    for copy in (home_ac, home_mc, home_rp):
        copy.wait()
    for d in range(1, blks):
        src = lax.rem(b + d, blks)
        remote(acol_h, ac_v.at[src], ac_send.at[d], ac_recv.at[src], (r, b)).wait_recv()
    for k in (0, 2):
        remote(mcol_h.at[t], mc_v.at[k], mc_send.at[k], mc_recv.at[k], (r, b)).wait_recv()
        remote(rpat_h.at[t], rp_v.at[k], rp_send.at[k], rp_recv.at[k], (r, b)).wait_recv()
    moves = [
        pltpu.make_async_copy(ac_v, ac_s, loc.at[2]),
        pltpu.make_async_copy(mc_v, mc_s, loc.at[3]),
        pltpu.make_async_copy(rp_v, rp_s, loc.at[4]),
    ]
    for copy in moves:
        copy.start()
    for copy in moves:
        copy.wait()

    row0 = own * x
    slots = blks * per

    def table_row(i, carry):
        pats = [rpat_s[t, row0 + i, p] for p in range(q2)]
        cands = [cand_s[t, row0 + i, c] for c in range(q2)]
        for p in range(q2):
            owner = scol_s[t, pats[p]]
            diag[q2 * i + p] = jnp.where(owner == rows * r + row0 + i, 1, 0)

        def table_slot(s, inner):
            col = ac_s[s // per, row0 + i, s % per]
            present = col >= 0
            w = lax.rem(col - rows * r + reach + total, total) - row0
            w = jnp.clip(w, 0, 2 * reach + own - 1)
            rel = w + row0
            side, line = lax.shift_right_logical(rel, rows.bit_length() - 1), rel & (rows - 1)
            mc = [mc_s[side, line, q] for q in range(qm)]
            rp = [rp_s[side, line, q] for q in range(q2)]
            for p in range(q2):
                at_m, at_r = jnp.int32(zero_m), jnp.int32(zero_r)
                for q in range(qm):
                    at_m = jnp.where(present & (mc[q] == pats[p]), w * qm + q, at_m)
                for q in range(q2):
                    at_r = jnp.where(present & (rp[q] == cands[p]), w * q2 + q, at_r)
                idx_m[(i * slots + s) * q2 + p] = at_m
                idx_r[(i * slots + s) * q2 + p] = at_r
            return inner

        return lax.fori_loop(0, slots, table_slot, carry)

    lax.fori_loop(0, own, table_row, 0)

    for k, d in enumerate((1, chips - 1) + tuple(range(2, chips - 1))):
        src = chip(d)
        remote(a_win.at[src], a_win.at[src], a_send.at[d], a_recv.at[src], (r, b)).wait_recv()
        swaps.append(remote(
            a_win.at[src], a_win.at[src], a_send.at[chips + 1 + k], a_recv.at[src], mate
        ))
        swaps[-1].start()
    for d in range(chips):
        src = CORES * across(d) + (1 - t)
        remote(a_win.at[src], a_win.at[src], a_send.at[0], a_recv.at[src], (r, b)).wait_recv()
    home_m.wait()
    for slot in range(2 * chips + 1):
        here = (slot >= chips - x) & (slot < 2 * chips - x)
        got = remote(
            mval_h.at[t, pl.ds(0, mq)], m_win.at[pl.ds(mq * slot, mq)],
            m_send.at[0], m_recv.at[slot], (r, b),
        )
        pl.when(jnp.logical_not(here))(got.wait_recv)

    def product(i, win, table):
        def step(k, acc):
            lhs = jnp.concatenate([a_win[k, i, s] for s in range(per)], axis=1)
            picks = []
            for s in range(per):
                at = (i * slots + k * per + s) * q2
                picks.append(jnp.concatenate([win[table[at + p]] for p in range(q2)], axis=1))
            rhs = jnp.concatenate(picks, axis=0)
            return acc + jnp.dot(lhs, rhs, preferred_element_type=jnp.float32)

        return lax.fori_loop(0, blks, step, jnp.zeros((n, q2 * n), jnp.float32))

    eye = (
        lax.broadcasted_iota(jnp.int32, (n, n), 0) == lax.broadcasted_iota(jnp.int32, (n, n), 1)
    ).astype(jnp.float32)

    def resid_row(i, carry):
        summed = product(i, m_win, idx_m)
        for p in range(q2):
            block = summed[:, n * p:n * (p + 1)] - diag[q2 * i + p].astype(jnp.float32) * eye
            r_win[rq * chips + q2 * i + p] = block.astype(r_win.dtype)
            r_turn[q2 * i + p] = block.T.astype(r_turn.dtype)
        return carry

    lax.fori_loop(0, own, resid_row, 0)

    mine = r_win.at[pl.ds(rq * chips, rq)]
    r_out = []
    for d in (1, chips - 1) + tuple(range(2, chips - 1)):
        slot = chips + x - across(d)
        r_out.append((None, remote(
            mine, r_win.at[pl.ds(rq * slot, rq)], r_send.at[d], r_recv.at[slot], (r, chip(d))
        )))
    for j in range(chips):
        for cond, slot, ring, k in (
            (j <= x, x - j, up, 1),
            (j >= x, 2 * chips + x - j, down, 2),
        ):
            safe = jnp.clip(slot, 0, 2 * chips)
            r_out.append((cond, remote(
                mine, r_win.at[pl.ds(rq * safe, rq)], r_send.at[chips * k + j], r_recv.at[safe],
                (ring, CORES * j + t),
            )))
    for cond, copy in r_out:
        if cond is None:
            copy.start()
        else:
            pl.when(cond)(copy.start)

    width = n // blks
    home_o = pltpu.make_async_copy(
        r_turn.at[:, pl.ds(width * b, width), :], o_res.at[t, pl.ds(rq * x, rq)], loc.at[0]
    )
    home_o.start()
    o_out = []
    for d in range(1, blks):
        to = lax.rem(b + d, blks)
        o_out.append(remote(
            r_turn.at[:, pl.ds(width * to, width), :], o_res.at[t, pl.ds(rq * x, rq)],
            o_send.at[d], o_recv.at[b], (r, to),
        ))
        o_out[-1].start()

    for slot in range(2 * chips + 1):
        if slot != chips:
            remote(
                mine, r_win.at[pl.ds(rq * slot, rq)], r_send.at[0], r_recv.at[slot], (r, b)
            ).wait_recv()

    def score_row(i, carry):
        proj = product(i, r_win, idx_r)
        means = jnp.sum(proj * proj, axis=0, keepdims=True) * (1.0 / n)
        for c in range(q2):
            sc_own[pl.ds(q2 * i + c, 1), :] = means[:, n * c:n * (c + 1)]
        return carry

    lax.fori_loop(0, own, score_row, 0)

    home_s = pltpu.make_async_copy(sc_own, o_sc.at[t, x], loc.at[1])
    home_s.start()
    s_out = []
    for d in range(1, blks):
        to = lax.rem(b + d, blks)
        s_out.append(remote(
            sc_own, o_sc.at[t, x], s_send.at[d], s_recv.at[b], (r, to)
        ))
        s_out[-1].start()

    for d in range(1, blks):
        src = lax.rem(b + d, blks)
        sx, st = src // CORES, src % CORES
        remote(
            r_turn.at[:, pl.ds(0, width), :], o_res.at[st, pl.ds(rq * sx, rq)],
            o_send.at[d], o_recv.at[src], (r, b),
        ).wait_recv()
        remote(sc_own, o_sc.at[st, sx], s_send.at[d], s_recv.at[src], (r, b)).wait_recv()
    home_o.wait()
    home_s.wait()
    for copy in ints + list(a_out.values()) + swaps + o_out + s_out:
        copy.wait_send()
    for cond, copy in m_out + r_out:
        if cond is None:
            copy.wait_send()
        else:
            pl.when(cond)(copy.wait_send)


def on_device(rings, blks, acol, aval, mcol, mval, rpat, scol, cand):
    rows, per, n, _ = aval.shape
    slabs, _, qm = mcol.shape
    q2 = rpat.shape[2]
    chips = blks // CORES
    own = rows // chips
    window = 2 * rows + own
    dims = (rings, blks, rows, own, per, qm, q2, n)
    width = n // blks
    smem = pl.BlockSpec(memory_space=pltpu.SMEM)
    anywhere = pl.BlockSpec(memory_space=pl.ANY)
    dma = pltpu.SemaphoreType.DMA
    slots = blks * per
    res, sc = pl.pallas_call(
        functools.partial(kernel, dims),
        out_shape=(
            jax.ShapeDtypeStruct((slabs, rows * q2, width, n), jnp.bfloat16),
            jax.ShapeDtypeStruct((slabs, chips, own * q2, n), jnp.float32),
        ),
        in_specs=[smem] * 3 + [anywhere] * 5,
        out_specs=(anywhere, anywhere),
        scratch_shapes=[
            pltpu.VMEM((blks, own, per, n, n), jnp.bfloat16),
            pltpu.VMEM((window * qm + 1, n, n), jnp.bfloat16),
            pltpu.VMEM((window * q2 + 1, n, n), jnp.bfloat16),
            pltpu.VMEM((own * q2, n, n), jnp.bfloat16),
            pltpu.VMEM((own * q2, n), jnp.float32),
            pltpu.VMEM((blks, rows, per), jnp.int32),
            pltpu.VMEM((3, rows, qm), jnp.int32),
            pltpu.VMEM((3, rows, q2), jnp.int32),
            pltpu.SMEM((blks, rows, per), jnp.int32),
            pltpu.SMEM((3, rows, qm), jnp.int32),
            pltpu.SMEM((3, rows, q2), jnp.int32),
            pltpu.SMEM((own * slots * q2,), jnp.int32),
            pltpu.SMEM((own * slots * q2,), jnp.int32),
            pltpu.SMEM((own * q2,), jnp.int32),
            dma((2 * chips,)), dma((blks,)),
            dma((2 * chips,)), dma((2 * chips + 1,)),
            dma((3 * chips,)), dma((2 * chips + 1,)),
            dma((blks,)), dma((blks,)), dma((3,)), dma((3,)), dma((3,)), dma((3,)),
            dma((blks,)), dma((blks,)), dma((blks,)), dma((blks,)), dma((5,)),
        ],
        compiler_params=pltpu.CompilerParams(
            collective_id=0, has_side_effects=True, vmem_limit_bytes=40 * 2**20
        ),
    )(
        scol, cand, rpat, acol, mcol, rpat, aval,
        mval.reshape(slabs, rows * qm, n, n),
    )
    start = lax.axis_index("blk") * width
    resid = res.reshape(slabs, rows, q2, width, n).swapaxes(3, 4)
    scores = lax.dynamic_slice_in_dim(sc, start, width, 3).reshape(slabs, rows, q2, width)
    return resid, scores


def solution(mesh):
    placed = (
        P("rows", "blk"),
        P("rows", "blk", None, None),
        P(None, "rows", None),
        P(None, "rows", None, None, None),
        P(None, "rows", None),
        P(),
        P(None, "rows", None),
    )
    return jax.shard_map(
        functools.partial(on_device, mesh.shape["rows"], mesh.shape["blk"]),
        mesh=mesh,
        in_specs=placed,
        out_specs=(P(None, "rows", None, None, "blk"), P(None, "rows", None, "blk")),
        check_vma=False,
    )
```

```python
import functools

import jax
import jax.numpy as jnp
from jax import lax
from jax.experimental import pallas as pl
from jax.experimental.pallas import tpu as pltpu
from jax.sharding import PartitionSpec as P

MESH = pl.DeviceIdType.MESH
CORES = 2


def kernel(
    dims,
    scol_h, cand_h, rpat_h, acol_h, mcol_h, aval_h, mval_h,
    o_res, o_sc,
    a_win, m_win, r_win, r_turn, sc_own, ac_v, mc_v, rp_v,
    ac_s, mc_s, rp_s, scol_s, cand_s, idx_m, idx_r, diag,
    a_send, a_recv, m_send, m_recv, r_send, r_recv,
    ac_send, ac_recv, mc_send, mc_recv, rp_send, rp_recv,
    o_send, o_recv, s_send, s_recv, h_send, h_recv, loc,
):
    rings, blks, rows, own, per, qm, q2, n = dims
    chips = blks // CORES
    reach = rows
    total = rings * rows
    r, b = lax.axis_index("rows"), lax.axis_index("blk")
    x, t = b // CORES, b % CORES
    up, down = lax.rem(r + 1, rings), lax.rem(r + rings - 1, rings)
    mate = (r, CORES * x + (1 - t))
    mq, rq = own * qm, own * q2
    zero_m, zero_r = m_win.shape[0] - 1, r_win.shape[0] - 1

    def remote(src, dst, send, recv, where):
        return pltpu.make_async_remote_copy(
            src_ref=src, dst_ref=dst, send_sem=send, recv_sem=recv,
            device_id=where, device_id_type=MESH,
        )

    def across(d):
        return lax.rem(x + d, chips)

    def chip(d):
        return CORES * across(d) + t

    home_a = pltpu.make_async_copy(aval_h.at[pl.ds(own * x, own)], a_win.at[b], loc.at[0])
    home_m = pltpu.make_async_copy(
        mval_h.at[t], m_win.at[pl.ds(mq * (chips - x), mq * chips)], loc.at[1]
    )
    home_ac = pltpu.make_async_copy(acol_h, ac_v.at[b], loc.at[2])
    home_mc = pltpu.make_async_copy(mcol_h.at[t], mc_v.at[1], loc.at[3])
    home_rp = pltpu.make_async_copy(rpat_h.at[t], rp_v.at[1], loc.at[4])
    home_sc = pltpu.make_async_copy(scol_h, scol_s, loc.at[5])
    home_ca = pltpu.make_async_copy(cand_h, cand_s, loc.at[6])

    barrier = pltpu.get_barrier_semaphore()
    for ring in (up, down):
        pl.semaphore_signal(barrier, inc=1, device_id=(ring, b), device_id_type=MESH)
    for d in range(1, blks):
        pl.semaphore_signal(
            barrier, inc=1, device_id=(r, lax.rem(b + d, blks)), device_id_type=MESH
        )
    for copy in (home_ac, home_mc, home_rp, home_sc, home_ca, home_a, home_m):
        copy.start()
    m_win[zero_m] = jnp.zeros((n, n), m_win.dtype)
    r_win[zero_r] = jnp.zeros((n, n), r_win.dtype)
    pl.semaphore_wait(barrier, blks - 1 + 2)

    ints = []
    for d in range(1, blks):
        to = lax.rem(b + d, blks)
        ints.append(remote(acol_h, ac_v.at[b], ac_send.at[d], ac_recv.at[b], (r, to)))
    for k, ring in ((0, up), (2, down)):
        ints.append(remote(mcol_h.at[t], mc_v.at[k], mc_send.at[k], mc_recv.at[k], (ring, b)))
        ints.append(remote(rpat_h.at[t], rp_v.at[k], rp_send.at[k], rp_recv.at[k], (ring, b)))
    for copy in ints:
        copy.start()

    last = chips - 1
    m_out = []
    for k in range(chips):
        for cond, j, slot, ring, side in (
            ((x <= last - k) & ((x > 0) | (k > 0)), last - k, last - k - x, up, 0),
            ((x >= k) & ((x < last) | (k > 0)), k, 2 * chips + k - x, down, 1),
        ):
            safe = jnp.clip(slot, 0, 2 * chips)
            m_out.append((cond, remote(
                mval_h.at[t, pl.ds(mq * j, mq)], m_win.at[pl.ds(mq * safe, mq)],
                m_send.at[chips * side + k], m_recv.at[safe], (ring, b),
            )))
    for cond, copy in m_out:
        pl.when(cond)(copy.start)
    a_out = {}
    for d in (1, chips - 1) + tuple(range(2, chips - 1)):
        a_out[d] = remote(
            aval_h.at[pl.ds(own * across(d), own)], a_win.at[b],
            a_send.at[d], a_recv.at[b], (r, chip(d)),
        )
        a_out[d].start()
    home_a.wait()
    swaps = [remote(a_win.at[b], a_win.at[b], a_send.at[chips], a_recv.at[b], mate)]
    swaps[0].start()

    for copy in (home_ac, home_mc, home_rp, home_sc, home_ca):
        copy.wait()
    for d in range(1, blks):
        src = lax.rem(b + d, blks)
        remote(acol_h, ac_v.at[src], ac_send.at[d], ac_recv.at[src], (r, b)).wait_recv()
    for k in (0, 2):
        remote(mcol_h.at[t], mc_v.at[k], mc_send.at[k], mc_recv.at[k], (r, b)).wait_recv()
        remote(rpat_h.at[t], rp_v.at[k], rp_send.at[k], rp_recv.at[k], (r, b)).wait_recv()
    moves = [
        pltpu.make_async_copy(ac_v, ac_s, loc.at[2]),
        pltpu.make_async_copy(mc_v, mc_s, loc.at[3]),
        pltpu.make_async_copy(rp_v, rp_s, loc.at[4]),
    ]
    for copy in moves:
        copy.start()
    for copy in moves:
        copy.wait()

    row0 = own * x
    slots = blks * per

    def table_row(i, carry):
        pats = [rp_s[1, p, row0 + i] for p in range(q2)]
        cands = [cand_s[t, c, row0 + i] for c in range(q2)]
        for p in range(q2):
            owner = scol_s[t, pats[p]]
            diag[q2 * i + p] = jnp.where(owner == rows * r + row0 + i, 1, 0)

        def table_slot(s, inner):
            col = ac_s[s // per, s % per, row0 + i]
            present = col >= 0
            w = lax.rem(col - rows * r + reach + total, total) - row0
            w = jnp.clip(w, 0, 2 * reach + own - 1)
            rel = w + row0
            side, line = lax.shift_right_logical(rel, rows.bit_length() - 1), rel & (rows - 1)
            mc = [mc_s[side, q, line] for q in range(qm)]
            rp = [rp_s[side, q, line] for q in range(q2)]
            for p in range(q2):
                at_m, at_r = jnp.int32(zero_m), jnp.int32(zero_r)
                for q in range(qm):
                    at_m = jnp.where(present & (mc[q] == pats[p]), w * qm + q, at_m)
                for q in range(q2):
                    at_r = jnp.where(present & (rp[q] == cands[p]), w * q2 + q, at_r)
                idx_m[(i * slots + s) * q2 + p] = at_m
                idx_r[(i * slots + s) * q2 + p] = at_r
            return inner

        return lax.fori_loop(0, slots, table_slot, carry)

    lax.fori_loop(0, own, table_row, 0)

    odd = lax.rem(x, 2) == 1
    half, hb = x // 2, mq // 2
    src_slot = jnp.where(odd, last - x, 2 * chips - x)
    dst_slot = jnp.where(odd, last, chips + 1)
    dst_chip = jnp.where(odd, 0, last)

    def m_wait(slot):
        remote(
            mval_h.at[t, pl.ds(0, mq)], m_win.at[pl.ds(mq * slot, mq)],
            m_send.at[0], m_recv.at[slot], (r, b),
        ).wait_recv()

    m_wait(src_slot)
    relay = remote(
        m_win.at[pl.ds(mq * src_slot + hb * half, hb)],
        m_win.at[pl.ds(mq * dst_slot + hb * half, hb)],
        h_send.at[0], h_recv.at[half], (r, CORES * dst_chip + t),
    )
    relay.start()

    for k, d in enumerate((1, chips - 1) + tuple(range(2, chips - 1))):
        src = chip(d)
        remote(a_win.at[src], a_win.at[src], a_send.at[d], a_recv.at[src], (r, b)).wait_recv()
        swaps.append(remote(
            a_win.at[src], a_win.at[src], a_send.at[chips + 1 + k], a_recv.at[src], mate
        ))
        swaps[-1].start()
    for d in range(chips):
        src = CORES * across(d) + (1 - t)
        remote(a_win.at[src], a_win.at[src], a_send.at[0], a_recv.at[src], (r, b)).wait_recv()
    home_m.wait()
    edge = (x == 0) | (x == last)
    far = jnp.where(x == 0, last, chips + 1)
    for slot in range(2 * chips + 1):
        here = (slot >= chips - x) & (slot < 2 * chips - x)
        skip = here | (slot == src_slot) | (edge & (slot == far))
        pl.when(jnp.logical_not(skip))(functools.partial(m_wait, slot))

    @pl.when(edge)
    def _():
        for h in range(2):
            part = m_win.at[pl.ds(mq * far + hb * h, hb)]
            remote(part, part, h_send.at[0], h_recv.at[h], (r, b)).wait_recv()

    def product(i, win, table):
        acc = None
        for k in range(blks):
            lhs = jnp.concatenate([a_win[k, i, s] for s in range(per)], axis=1)
            picks = []
            for s in range(per):
                at = (i * slots + k * per + s) * q2
                picks.append(jnp.concatenate([win[table[at + p]] for p in range(q2)], axis=1))
            rhs = jnp.concatenate(picks, axis=0)
            part = jnp.dot(lhs, rhs, preferred_element_type=jnp.float32)
            acc = part if acc is None else acc + part
        return acc

    eye = (
        lax.broadcasted_iota(jnp.int32, (n, n), 0) == lax.broadcasted_iota(jnp.int32, (n, n), 1)
    ).astype(jnp.float32)

    def resid_row(i, carry):
        summed = product(i, m_win, idx_m)
        for p in range(q2):
            block = summed[:, n * p:n * (p + 1)] - diag[q2 * i + p].astype(jnp.float32) * eye
            r_win[rq * chips + q2 * i + p] = block.astype(r_win.dtype)
            r_turn[q2 * i + p] = block.T.astype(r_turn.dtype)
        return carry

    left, right = lax.rem(x + last, chips), lax.rem(x + 1, chips)
    by_left, by_right = (r, CORES * left + t), (r, CORES * right + t)
    above, below = (up, b), (down, b)
    rh = rq // 2
    r_all = []

    def piece(slot, h):
        return r_win.at[pl.ds(rq * slot + rh * h, rh)]

    def give(slot, h, to_slot, where, cond=None):
        if cond is not None:
            to_slot = jnp.clip(to_slot, 0, 2 * chips)
        copy = remote(
            piece(slot, h), piece(to_slot, h), r_send.at[len(r_all)],
            r_recv.at[2 * to_slot + h], where,
        )
        r_all.append((cond, copy))
        if cond is None:
            copy.start()
        else:
            pl.when(cond)(copy.start)

    def take(slot, h, cond=None):
        def wait():
            remote(
                piece(slot, h), piece(slot, h), r_send.at[0], r_recv.at[2 * slot + h], (r, b)
            ).wait_recv()

        if cond is None:
            wait()
        else:
            pl.when(cond)(wait)

    for h in range(2):
        lax.fori_loop(own // 2 * h, own // 2 * (h + 1), resid_row, 0)
        give(chips, h, chips + x - right, by_right)
        give(chips, h, chips + x - left, by_left)
        give(chips, h, 0, above)
        give(chips, h, 2 * chips, below)

    width = n // blks
    home_o = pltpu.make_async_copy(
        r_turn.at[:, pl.ds(width * b, width), :], o_res.at[t, pl.ds(rq * x, rq)], loc.at[0]
    )
    home_o.start()
    o_out = []
    for d in range(1, blks):
        to = lax.rem(b + d, blks)
        o_out.append(remote(
            r_turn.at[:, pl.ds(width * to, width), :], o_res.at[t, pl.ds(rq * x, rq)],
            o_send.at[d], o_recv.at[b], (r, to),
        ))
        o_out[-1].start()

    at_left, at_right = chips + left - x, chips + right - x
    for h in range(2):
        take(at_left, h)
        if h == 0:
            give(at_left, h, chips + left - right, by_right)
        give(at_left, h, 2 * chips - 1, below, x >= 1)
        take(at_right, h)
        if h == 1:
            give(at_right, h, chips + right - left, by_left)
        give(at_right, h, 1, above, x <= last - 1)
        take(0, h)
        give(0, h, last, by_right, x == last)
        take(2 * chips, h)
        give(2 * chips, h, chips + 1, by_left, x == 0)
    inner = (x >= 1) & (x <= last - 1)
    for h in range(2):
        take(1, h, x <= last - 1)
        give(1, h, 2, by_left, inner)
        take(2 * chips - 1, h, x >= 1)
        give(2 * chips - 1, h, 2 * chips - 2, by_right, inner)
    for h in range(2):
        take(jnp.where(x < 2, chips + 2, chips - 2), h)
        take(2, h, x < 2)
        take(3, h, x == 0)
        take(2 * chips - 2, h, x >= 2)
        take(chips + 1, h, x == last)

    def score_row(i, carry):
        proj = product(i, r_win, idx_r)
        means = jnp.sum(proj * proj, axis=0, keepdims=True) * (1.0 / n)
        for c in range(q2):
            sc_own[pl.ds(q2 * i + c, 1), :] = means[:, n * c:n * (c + 1)]
        return carry

    lax.fori_loop(0, own, score_row, 0)

    home_s = pltpu.make_async_copy(sc_own, o_sc.at[t, x], loc.at[1])
    home_s.start()
    s_out = []
    for d in range(1, blks):
        to = lax.rem(b + d, blks)
        s_out.append(remote(
            sc_own, o_sc.at[t, x], s_send.at[d], s_recv.at[b], (r, to)
        ))
        s_out[-1].start()

    for d in range(1, blks):
        src = lax.rem(b + d, blks)
        sx, st = src // CORES, src % CORES
        remote(
            r_turn.at[:, pl.ds(0, width), :], o_res.at[st, pl.ds(rq * sx, rq)],
            o_send.at[d], o_recv.at[src], (r, b),
        ).wait_recv()
        remote(sc_own, o_sc.at[st, sx], s_send.at[d], s_recv.at[src], (r, b)).wait_recv()
    home_o.wait()
    home_s.wait()
    for copy in ints + list(a_out.values()) + swaps + [relay] + o_out + s_out:
        copy.wait_send()
    for cond, copy in m_out + r_all:
        if cond is None:
            copy.wait_send()
        else:
            pl.when(cond)(copy.wait_send)


def on_device(rings, blks, acol, aval, mcol, mval, rpat, scol, cand):
    rows, per, n, _ = aval.shape
    slabs, _, qm = mcol.shape
    q2 = rpat.shape[2]
    chips = blks // CORES
    own = rows // chips
    window = 2 * rows + own
    dims = (rings, blks, rows, own, per, qm, q2, n)
    width = n // blks
    anywhere = pl.BlockSpec(memory_space=pl.ANY)
    dma = pltpu.SemaphoreType.DMA
    slots = blks * per
    res, sc = pl.pallas_call(
        functools.partial(kernel, dims),
        out_shape=(
            jax.ShapeDtypeStruct((slabs, rows * q2, width, n), jnp.bfloat16),
            jax.ShapeDtypeStruct((slabs, chips, own * q2, n), jnp.float32),
        ),
        in_specs=[anywhere] * 7,
        out_specs=(anywhere, anywhere),
        scratch_shapes=[
            pltpu.VMEM((blks, own, per, n, n), jnp.bfloat16),
            pltpu.VMEM((window * qm + 1, n, n), jnp.bfloat16),
            pltpu.VMEM((window * q2 + 1, n, n), jnp.bfloat16),
            pltpu.VMEM((own * q2, n, n), jnp.bfloat16),
            pltpu.VMEM((own * q2, n), jnp.float32),
            pltpu.VMEM((blks, per, rows), jnp.int32),
            pltpu.VMEM((3, qm, rows), jnp.int32),
            pltpu.VMEM((3, q2, rows), jnp.int32),
            pltpu.SMEM((blks, per, rows), jnp.int32),
            pltpu.SMEM((3, qm, rows), jnp.int32),
            pltpu.SMEM((3, q2, rows), jnp.int32),
            pltpu.SMEM(scol.shape, jnp.int32),
            pltpu.SMEM((slabs, q2, rows), jnp.int32),
            pltpu.SMEM((own * slots * q2,), jnp.int32),
            pltpu.SMEM((own * slots * q2,), jnp.int32),
            pltpu.SMEM((own * q2,), jnp.int32),
            dma((2 * chips,)), dma((blks,)),
            dma((2 * chips,)), dma((2 * chips + 1,)),
            dma((26,)), dma((4 * chips + 2,)),
            dma((blks,)), dma((blks,)), dma((3,)), dma((3,)), dma((3,)), dma((3,)),
            dma((blks,)), dma((blks,)), dma((blks,)), dma((blks,)),
            dma((1,)), dma((2,)), dma((7,)),
        ],
        compiler_params=pltpu.CompilerParams(
            collective_id=0, has_side_effects=True, vmem_limit_bytes=67043328
        ),
    )(
        scol, cand.swapaxes(1, 2), rpat.swapaxes(1, 2), acol.T, mcol.swapaxes(1, 2), aval,
        mval.reshape(slabs, rows * qm, n, n),
    )
    start = lax.axis_index("blk") * width
    resid = res.reshape(slabs, rows, q2, width, n).swapaxes(3, 4)
    scores = lax.dynamic_slice_in_dim(sc, start, width, 3).reshape(slabs, rows, q2, width)
    return resid, scores


def solution(mesh):
    placed = (
        P("rows", "blk"),
        P("rows", "blk", None, None),
        P(None, "rows", None),
        P(None, "rows", None, None, None),
        P(None, "rows", None),
        P(),
        P(None, "rows", None),
    )
    return jax.shard_map(
        functools.partial(on_device, mesh.shape["rows"], mesh.shape["blk"]),
        mesh=mesh,
        in_specs=placed,
        out_specs=(P(None, "rows", None, None, "blk"), P(None, "rows", None, "blk")),
        check_vma=False,
    )
```

```python
import functools

import jax
import jax.numpy as jnp
from jax import lax
from jax.experimental import pallas as pl
from jax.experimental.pallas import tpu as pltpu
from jax.sharding import PartitionSpec as P

MESH = pl.DeviceIdType.MESH
CORES = 2


def kernel(
    dims,
    scol_h, cand_h, rpat_h, acol_h, mcol_h, aval_h, mval_h,
    o_res, o_sc,
    a_win, m_win, r_win, r_turn, sc_own, ac_v, mc_v, rp_v,
    ac_s, mc_s, rp_s, scol_s, cand_s, idx_m, idx_r, diag,
    a_send, a_recv, m_send, m_recv, r_send, r_recv,
    ac_send, ac_recv, mc_send, mc_recv, rp_send, rp_recv,
    o_send, o_recv, s_send, s_recv, h_send, h_recv, loc,
):
    rings, blks, rows, own, per, qm, q2, n = dims
    chips = blks // CORES
    reach = rows
    total = rings * rows
    r, b = lax.axis_index("rows"), lax.axis_index("blk")
    x, t = b // CORES, b % CORES
    up, down = lax.rem(r + 1, rings), lax.rem(r + rings - 1, rings)
    mate = (r, CORES * x + (1 - t))
    mq, rq = own * qm, own * q2
    zero_m, zero_r = m_win.shape[0] - 1, r_win.shape[0] - 1

    def remote(src, dst, send, recv, where):
        return pltpu.make_async_remote_copy(
            src_ref=src, dst_ref=dst, send_sem=send, recv_sem=recv,
            device_id=where, device_id_type=MESH,
        )

    def across(d):
        return lax.rem(x + d, chips)

    def chip(d):
        return CORES * across(d) + t

    home_a = pltpu.make_async_copy(aval_h.at[pl.ds(own * x, own)], a_win.at[b], loc.at[0])
    home_m = pltpu.make_async_copy(
        mval_h.at[t], m_win.at[pl.ds(mq * (chips - x), mq * chips)], loc.at[1]
    )
    home_ac = pltpu.make_async_copy(acol_h, ac_v.at[b], loc.at[2])
    home_mc = pltpu.make_async_copy(mcol_h.at[t], mc_v.at[1], loc.at[3])
    home_rp = pltpu.make_async_copy(rpat_h.at[t], rp_v.at[1], loc.at[4])
    home_sc = pltpu.make_async_copy(scol_h, scol_s, loc.at[5])
    home_ca = pltpu.make_async_copy(cand_h, cand_s, loc.at[6])

    barrier = pltpu.get_barrier_semaphore()
    for ring in (up, down):
        pl.semaphore_signal(barrier, inc=1, device_id=(ring, b), device_id_type=MESH)
    for d in range(1, blks):
        pl.semaphore_signal(
            barrier, inc=1, device_id=(r, lax.rem(b + d, blks)), device_id_type=MESH
        )
    for copy in (home_ac, home_mc, home_rp, home_sc, home_ca, home_a, home_m):
        copy.start()
    m_win[zero_m] = jnp.zeros((n, n), m_win.dtype)
    r_win[zero_r] = jnp.zeros((n, n), r_win.dtype)
    pl.semaphore_wait(barrier, blks - 1 + 2)

    ints = []
    for d in range(1, blks):
        to = lax.rem(b + d, blks)
        ints.append(remote(acol_h, ac_v.at[b], ac_send.at[d], ac_recv.at[b], (r, to)))
    for k, ring in ((0, up), (2, down)):
        ints.append(remote(mcol_h.at[t], mc_v.at[k], mc_send.at[k], mc_recv.at[k], (ring, b)))
        ints.append(remote(rpat_h.at[t], rp_v.at[k], rp_send.at[k], rp_recv.at[k], (ring, b)))
    for copy in ints:
        copy.start()

    last = chips - 1
    m_out = []
    mh, hr = mq // 2, own // 2
    for k in range(chips):
        for e in range(2):
            for cond, skip, j, h, slot, ring in (
                (x <= last - k, ((1, 0), (0, 0), (0, 1), (0, 2)), last - k, 1 - e, last - k - x, up),
                (x >= k, ((last - 1, 0), (last, 0), (last, 1), (last, 2)), k, e,
                 2 * chips + k - x, down),
            ):
                if k == 0 and e == 0:
                    cond &= (x != skip[0][0]) & (x != skip[1][0])
                elif k == 0 or (k == 1 and e == 0):
                    cond &= x != skip[1][0]
                safe = jnp.clip(slot, 0, 2 * chips)
                m_out.append((cond, remote(
                    mval_h.at[t, pl.ds(mq * j + mh * h, mh)],
                    m_win.at[pl.ds(mq * safe + mh * h, mh)],
                    m_send.at[len(m_out)], m_recv.at[2 * safe + h], (ring, b),
                )))
    for cond, copy in m_out:
        pl.when(cond)(copy.start)
    hops = (1, chips - 1) + tuple(range(2, chips - 1))
    a_all = []

    def a_part(src, g):
        return a_win.at[src, pl.ds(hr * g, hr)]

    def a_copy(source, src, g, where):
        copy = remote(
            source, a_part(src, g), a_send.at[len(a_all)], a_recv.at[blks * g + src], where
        )
        copy.start()
        a_all.append(copy)

    def a_wait(src, g):
        remote(
            a_part(src, g), a_part(src, g), a_send.at[0], a_recv.at[blks * g + src], (r, b)
        ).wait_recv()

    for g in range(2):
        for d in hops:
            a_copy(aval_h.at[pl.ds(own * across(d) + hr * g, hr)], b, g, (r, chip(d)))
    home_a.wait()
    for g in range(2):
        a_copy(a_part(b, g), b, g, mate)

    for copy in (home_ac, home_mc, home_rp, home_sc, home_ca):
        copy.wait()
    for d in range(1, blks):
        src = lax.rem(b + d, blks)
        remote(acol_h, ac_v.at[src], ac_send.at[d], ac_recv.at[src], (r, b)).wait_recv()
    for k in (0, 2):
        remote(mcol_h.at[t], mc_v.at[k], mc_send.at[k], mc_recv.at[k], (r, b)).wait_recv()
        remote(rpat_h.at[t], rp_v.at[k], rp_send.at[k], rp_recv.at[k], (r, b)).wait_recv()
    moves = [
        pltpu.make_async_copy(ac_v, ac_s, loc.at[2]),
        pltpu.make_async_copy(mc_v, mc_s, loc.at[3]),
        pltpu.make_async_copy(rp_v, rp_s, loc.at[4]),
    ]
    for copy in moves:
        copy.start()
    for copy in moves:
        copy.wait()

    row0 = own * x
    slots = blks * per

    def table_row(i, carry):
        pats = [rp_s[1, p, row0 + i] for p in range(q2)]
        cands = [cand_s[t, c, row0 + i] for c in range(q2)]
        for p in range(q2):
            owner = scol_s[t, pats[p]]
            diag[q2 * i + p] = jnp.where(owner == rows * r + row0 + i, 1, 0)

        def table_slot(s, inner):
            col = ac_s[s // per, s % per, row0 + i]
            present = col >= 0
            w = lax.rem(col - rows * r + reach + total, total) - row0
            w = jnp.clip(w, 0, 2 * reach + own - 1)
            rel = w + row0
            side, line = lax.shift_right_logical(rel, rows.bit_length() - 1), rel & (rows - 1)
            mc = [mc_s[side, q, line] for q in range(qm)]
            rp = [rp_s[side, q, line] for q in range(q2)]
            for p in range(q2):
                at_m, at_r = jnp.int32(zero_m), jnp.int32(zero_r)
                for q in range(qm):
                    at_m = jnp.where(present & (mc[q] == pats[p]), w * qm + q, at_m)
                for q in range(q2):
                    at_r = jnp.where(present & (rp[q] == cands[p]), w * q2 + q, at_r)
                idx_m[(i * slots + s) * q2 + p] = at_m
                idx_r[(i * slots + s) * q2 + p] = at_r
            return inner

        return lax.fori_loop(0, slots, table_slot, carry)

    lax.fori_loop(0, own, table_row, 0)

    left, right = lax.rem(x + last, chips), lax.rem(x + 1, chips)
    by_left, by_right = (r, CORES * left + t), (r, CORES * right + t)
    above, below = (up, b), (down, b)
    inner = (x >= 1) & (x <= last - 1)

    def m_rows(slot, first, count):
        return m_win.at[pl.ds(mq * slot + qm * first, qm * count)]

    def m_take(slot, h):
        part = m_rows(slot, hr * h, hr)
        remote(part, part, m_send.at[0], m_recv.at[2 * slot + h], (r, b)).wait_recv()

    relays = []
    for cond, needs, slots_of, rows_of, sem, where in (
        (x == last, ((0, 1), (0, 0)), (0, last), (1, own - 1), h_recv.at[1], by_right),
        (x == 0, ((2 * chips, 0), (2 * chips, 1)), (2 * chips, chips + 1), (0, own - 1),
         h_recv.at[1], by_left),
        (x == 1, ((2, 0),), (2, last), (0, 1), h_recv.at[0], by_left),
        (x == last - 1, ((2 * chips - 2, 1),), (2 * chips - 2, chips + 1), (own - 1, 1),
         h_recv.at[0], by_right),
        (inner, ((1, 1),), (1, 2), (hr, hr), m_recv.at[2 * 2 + 1], by_left),
        (inner, ((2 * chips - 1, 0),), (2 * chips - 1, 2 * chips - 2), (0, hr),
         m_recv.at[2 * (2 * chips - 2)], by_right),
    ):
        copy = remote(
            m_rows(slots_of[0], *rows_of), m_rows(slots_of[1], *rows_of),
            h_send.at[len(relays)], sem, where,
        )
        relays.append((cond, copy))

        def pass_on(needs=needs, copy=copy):
            for slot, h in needs:
                m_take(slot, h)
            copy.start()

        pl.when(cond)(pass_on)

    def a_swap(g):
        for d in hops:
            a_wait(chip(d), g)
            a_copy(a_part(chip(d), g), chip(d), g, mate)
        for d in range(chips):
            a_wait(CORES * across(d) + (1 - t), g)

    a_swap(0)
    home_m.wait()
    edge = (x == 0) | (x == last)
    for k in range(chips):
        for e in range(2):
            for cond, taken, slot, h in (
                (
                    k <= last - x,
                    ((x == last) & (k == 0)) | ((x == 1) & (k == 2) & (e == 1))
                    | (inner & (k == 1) & (e == 0)) | ((x == 0) & (k == last)),
                    k, 1 - e,
                ),
                (
                    k <= x,
                    ((x == 0) & (k == 0)) | ((x == last - 1) & (k == 2) & (e == 1))
                    | (inner & (k == 1) & (e == 0)) | ((x == last) & (k == last)),
                    2 * chips - k, e,
                ),
            ):
                pl.when(cond & jnp.logical_not(taken))(functools.partial(m_take, slot, h))

    def far_take(slot, one, rest):
        for k, span in ((0, (one, 1)), (1, (rest, own - 1))):
            part = m_rows(slot, *span)
            remote(part, part, h_send.at[0], h_recv.at[k], (r, b)).wait_recv()

    pl.when(x == 0)(lambda: far_take(last, 0, 1))
    pl.when(x == last)(lambda: far_take(chips + 1, own - 1, 0))

    def product(i, win, table):
        acc = None
        for k in range(blks):
            lhs = jnp.concatenate([a_win[k, i, s] for s in range(per)], axis=1)
            picks = []
            for s in range(per):
                at = (i * slots + k * per + s) * q2
                picks.append(jnp.concatenate([win[table[at + p]] for p in range(q2)], axis=1))
            rhs = jnp.concatenate(picks, axis=0)
            part = jnp.dot(lhs, rhs, preferred_element_type=jnp.float32)
            acc = part if acc is None else acc + part
        return acc

    eye = (
        lax.broadcasted_iota(jnp.int32, (n, n), 0) == lax.broadcasted_iota(jnp.int32, (n, n), 1)
    ).astype(jnp.float32)

    def resid_row(i, carry):
        summed = product(i, m_win, idx_m)
        for p in range(q2):
            block = summed[:, n * p:n * (p + 1)] - diag[q2 * i + p].astype(jnp.float32) * eye
            r_win[rq * chips + q2 * i + p] = block.astype(r_win.dtype)
            r_turn[q2 * i + p] = block.T.astype(r_turn.dtype)
        return carry

    rh = rq // 2
    r_all = []

    def piece(slot, h):
        return r_win.at[pl.ds(rq * slot + rh * h, rh)]

    def give(slot, h, to_slot, where, cond=None):
        if cond is not None:
            to_slot = jnp.clip(to_slot, 0, 2 * chips)
        copy = remote(
            piece(slot, h), piece(to_slot, h), r_send.at[len(r_all)],
            r_recv.at[2 * to_slot + h], where,
        )
        r_all.append((cond, copy))
        if cond is None:
            copy.start()
        else:
            pl.when(cond)(copy.start)

    def take(slot, h, cond=None):
        def wait():
            remote(
                piece(slot, h), piece(slot, h), r_send.at[0], r_recv.at[2 * slot + h], (r, b)
            ).wait_recv()

        if cond is None:
            wait()
        else:
            pl.when(cond)(wait)

    for h in range(2):
        if h == 1:
            a_swap(1)
        lax.fori_loop(own // 2 * h, own // 2 * (h + 1), resid_row, 0)
        give(chips, h, chips + x - right, by_right)
        give(chips, h, chips + x - left, by_left)
        give(chips, h, 0, above)
        give(chips, h, 2 * chips, below)

    at_left, at_right = chips + left - x, chips + right - x
    for h in range(2):
        take(at_left, h)
        if h == 0:
            give(at_left, h, chips + left - right, by_right)
        give(at_left, h, 2 * chips - 1, below, x >= 1)
        take(at_right, h)
        if h == 1:
            give(at_right, h, chips + right - left, by_left)
        give(at_right, h, 1, above, x <= last - 1)
        take(0, h)
        give(0, h, last, by_right, x == last)
        take(2 * chips, h)
        give(2 * chips, h, chips + 1, by_left, x == 0)
    for h in range(2):
        take(1, h, x <= last - 1)
        give(1, h, 2, by_left, inner)
        take(2 * chips - 1, h, x >= 1)
        give(2 * chips - 1, h, 2 * chips - 2, by_right, inner)
    for h in range(2):
        take(jnp.where(x < 2, chips + 2, chips - 2), h)
        take(2, h, x < 2)
        take(3, h, x == 0)
        take(2 * chips - 2, h, x >= 2)
        take(chips + 1, h, x == last)

    width = n // blks
    home_o = pltpu.make_async_copy(
        r_turn.at[:, pl.ds(width * b, width), :], o_res.at[t, pl.ds(rq * x, rq)], loc.at[0]
    )
    home_o.start()
    o_out = []
    for d in range(1, blks):
        to = lax.rem(b + d, blks)
        o_out.append(remote(
            r_turn.at[:, pl.ds(width * to, width), :], o_res.at[t, pl.ds(rq * x, rq)],
            o_send.at[d], o_recv.at[b], (r, to),
        ))
        o_out[-1].start()

    def score_row(i, carry):
        proj = product(i, r_win, idx_r)
        means = jnp.sum(proj * proj, axis=0, keepdims=True) * (1.0 / n)
        for c in range(q2):
            sc_own[pl.ds(q2 * i + c, 1), :] = means[:, n * c:n * (c + 1)]
        return carry

    lax.fori_loop(0, own, score_row, 0)

    home_s = pltpu.make_async_copy(sc_own, o_sc.at[t, x], loc.at[1])
    home_s.start()
    s_out = []
    for d in range(1, blks):
        to = lax.rem(b + d, blks)
        s_out.append(remote(
            sc_own, o_sc.at[t, x], s_send.at[d], s_recv.at[b], (r, to)
        ))
        s_out[-1].start()

    for d in range(1, blks):
        src = lax.rem(b + d, blks)
        sx, st = src // CORES, src % CORES
        remote(
            r_turn.at[:, pl.ds(0, width), :], o_res.at[st, pl.ds(rq * sx, rq)],
            o_send.at[d], o_recv.at[src], (r, b),
        ).wait_recv()
        remote(sc_own, o_sc.at[st, sx], s_send.at[d], s_recv.at[src], (r, b)).wait_recv()
    home_o.wait()
    home_s.wait()
    for copy in ints + a_all + o_out + s_out:
        copy.wait_send()
    for cond, copy in m_out + relays + r_all:
        if cond is None:
            copy.wait_send()
        else:
            pl.when(cond)(copy.wait_send)


def on_device(rings, blks, acol, aval, mcol, mval, rpat, scol, cand):
    rows, per, n, _ = aval.shape
    slabs, _, qm = mcol.shape
    q2 = rpat.shape[2]
    chips = blks // CORES
    own = rows // chips
    window = 2 * rows + own
    dims = (rings, blks, rows, own, per, qm, q2, n)
    width = n // blks
    anywhere = pl.BlockSpec(memory_space=pl.ANY)
    dma = pltpu.SemaphoreType.DMA
    slots = blks * per
    res, sc = pl.pallas_call(
        functools.partial(kernel, dims),
        out_shape=(
            jax.ShapeDtypeStruct((slabs, rows * q2, width, n), jnp.bfloat16),
            jax.ShapeDtypeStruct((slabs, chips, own * q2, n), jnp.float32),
        ),
        in_specs=[anywhere] * 7,
        out_specs=(anywhere, anywhere),
        scratch_shapes=[
            pltpu.VMEM((blks, own, per, n, n), jnp.bfloat16),
            pltpu.VMEM((window * qm + 1, n, n), jnp.bfloat16),
            pltpu.VMEM((window * q2 + 1, n, n), jnp.bfloat16),
            pltpu.VMEM((own * q2, n, n), jnp.bfloat16),
            pltpu.VMEM((own * q2, n), jnp.float32),
            pltpu.VMEM((blks, per, rows), jnp.int32),
            pltpu.VMEM((3, qm, rows), jnp.int32),
            pltpu.VMEM((3, q2, rows), jnp.int32),
            pltpu.SMEM((blks, per, rows), jnp.int32),
            pltpu.SMEM((3, qm, rows), jnp.int32),
            pltpu.SMEM((3, q2, rows), jnp.int32),
            pltpu.SMEM(scol.shape, jnp.int32),
            pltpu.SMEM((slabs, q2, rows), jnp.int32),
            pltpu.SMEM((own * slots * q2,), jnp.int32),
            pltpu.SMEM((own * slots * q2,), jnp.int32),
            pltpu.SMEM((own * q2,), jnp.int32),
            dma((4 * chips,)), dma((2 * blks,)),
            dma((4 * chips,)), dma((4 * chips + 2,)),
            dma((26,)), dma((4 * chips + 2,)),
            dma((blks,)), dma((blks,)), dma((3,)), dma((3,)), dma((3,)), dma((3,)),
            dma((blks,)), dma((blks,)), dma((blks,)), dma((blks,)),
            dma((6,)), dma((2,)), dma((7,)),
        ],
        compiler_params=pltpu.CompilerParams(
            collective_id=0, has_side_effects=True, vmem_limit_bytes=66 * 10**6
        ),
    )(
        scol, cand.swapaxes(1, 2), rpat.swapaxes(1, 2), acol.T, mcol.swapaxes(1, 2), aval,
        mval.reshape(slabs, rows * qm, n, n),
    )
    start = lax.axis_index("blk") * width
    resid = res.reshape(slabs, rows, q2, width, n).swapaxes(3, 4)
    scores = lax.dynamic_slice_in_dim(sc, start, width, 3).reshape(slabs, rows, q2, width)
    return resid, scores


def solution(mesh):
    placed = (
        P("rows", "blk"),
        P("rows", "blk", None, None),
        P(None, "rows", None),
        P(None, "rows", None, None, None),
        P(None, "rows", None),
        P(),
        P(None, "rows", None),
    )
    return jax.shard_map(
        functools.partial(on_device, mesh.shape["rows"], mesh.shape["blk"]),
        mesh=mesh,
        in_specs=placed,
        out_specs=(P(None, "rows", None, None, "blk"), P(None, "rows", None, "blk")),
        check_vma=False,
    )
```

```python
import functools

import jax
import jax.numpy as jnp
from jax import lax
from jax.experimental import pallas as pl
from jax.experimental.pallas import tpu as pltpu
from jax.sharding import PartitionSpec as P

MESH = pl.DeviceIdType.MESH
CORES = 2


def kernel(
    dims,
    scol_h, cand_h, rpat_h, acol_h, mcol_h, aval_h, mval_h,
    o_res, o_sc,
    a_win, m_win, r_win, r_turn, sc_own, ac_v, mc_v, rp_v,
    ac_s, mc_s, rp_s, scol_s, cand_s, idx_m, idx_r, diag,
    a_send, a_recv, m_send, m_recv, r_send, r_recv,
    ac_send, ac_recv, mc_send, mc_recv, rp_send, rp_recv,
    o_send, o_recv, s_send, s_recv, h_send, h_recv, loc,
):
    rings, blks, rows, own, per, qm, q2, n = dims
    chips = blks // CORES
    reach = rows
    total = rings * rows
    r, b = lax.axis_index("rows"), lax.axis_index("blk")
    x, t = b // CORES, b % CORES
    up, down = lax.rem(r + 1, rings), lax.rem(r + rings - 1, rings)
    mate = (r, CORES * x + (1 - t))
    mq, rq = own * qm, own * q2
    zero_m, zero_r = m_win.shape[0] - 1, r_win.shape[0] - 1

    def remote(src, dst, send, recv, where):
        return pltpu.make_async_remote_copy(
            src_ref=src, dst_ref=dst, send_sem=send, recv_sem=recv,
            device_id=where, device_id_type=MESH,
        )

    def across(d):
        return lax.rem(x + d, chips)

    def chip(d):
        return CORES * across(d) + t

    home_a = pltpu.make_async_copy(aval_h.at[pl.ds(own * x, own)], a_win.at[b], loc.at[0])
    home_m = pltpu.make_async_copy(
        mval_h.at[t], m_win.at[pl.ds(mq * (chips - x), mq * chips)], loc.at[1]
    )
    home_ac = pltpu.make_async_copy(acol_h, ac_v.at[b], loc.at[2])
    home_mc = pltpu.make_async_copy(mcol_h.at[t], mc_v.at[1], loc.at[3])
    home_rp = pltpu.make_async_copy(rpat_h.at[t], rp_v.at[1], loc.at[4])
    home_sc = pltpu.make_async_copy(scol_h, scol_s, loc.at[5])
    home_ca = pltpu.make_async_copy(cand_h, cand_s, loc.at[6])

    barrier = pltpu.get_barrier_semaphore()
    for ring in (up, down):
        pl.semaphore_signal(barrier, inc=1, device_id=(ring, b), device_id_type=MESH)
    for d in range(1, blks):
        pl.semaphore_signal(
            barrier, inc=1, device_id=(r, lax.rem(b + d, blks)), device_id_type=MESH
        )
    for copy in (home_ac, home_mc, home_rp, home_sc, home_ca, home_a, home_m):
        copy.start()
    m_win[zero_m] = jnp.zeros((n, n), m_win.dtype)
    r_win[zero_r] = jnp.zeros((n, n), r_win.dtype)
    pl.semaphore_wait(barrier, blks - 1 + 2)

    hr = own // 2
    hops = (1, chips - 1) + tuple(range(2, chips - 1))
    a_all = []
    a_rows = ((0, own - 1), (own - 1, 1))

    def a_part(src, g):
        return a_win.at[src, pl.ds(*a_rows[g])]

    def a_copy(source, src, g, where):
        copy = remote(
            source, a_part(src, g), a_send.at[len(a_all)], a_recv.at[blks * g + src], where
        )
        copy.start()
        a_all.append(copy)

    def a_wait(src, g):
        remote(
            a_part(src, g), a_part(src, g), a_send.at[0], a_recv.at[blks * g + src], (r, b)
        ).wait_recv()

    ints = []
    for d in range(1, blks):
        to = lax.rem(b + d, blks)
        ints.append(remote(acol_h, ac_v.at[b], ac_send.at[d], ac_recv.at[b], (r, to)))
    for k, ring in ((0, up), (2, down)):
        ints.append(remote(mcol_h.at[t], mc_v.at[k], mc_send.at[k], mc_recv.at[k], (ring, b)))
        ints.append(remote(rpat_h.at[t], rp_v.at[k], rp_send.at[k], rp_recv.at[k], (ring, b)))
    for copy in ints:
        copy.start()


    def a_start(g):
        for d in hops:
            a_copy(aval_h.at[pl.ds(own * across(d) + a_rows[g][0], a_rows[g][1])], b, g, (r, chip(d)))

    a_start(0)
    last = chips - 1
    m_out = []
    mh = mq // 2
    for k in range(chips):
        for e in range(2):
            for cond, skip, j, h, slot, ring in (
                (x <= last - k, ((1, 0), (0, 0), (0, 1), (0, 2)), last - k, 1 - e, last - k - x, up),
                (x >= k, ((last - 1, 0), (last, 0), (last, 1), (last, 2)), k, e,
                 2 * chips + k - x, down),
            ):
                if k == 0 and e == 0:
                    cond &= (x != skip[0][0]) & (x != skip[1][0])
                elif k == 0 or (k == 1 and e == 0):
                    cond &= x != skip[1][0]
                safe = jnp.clip(slot, 0, 2 * chips)
                m_out.append((cond, remote(
                    mval_h.at[t, pl.ds(mq * j + mh * h, mh)],
                    m_win.at[pl.ds(mq * safe + mh * h, mh)],
                    m_send.at[len(m_out)], m_recv.at[2 * safe + h], (ring, b),
                )))
    for cond, copy in m_out:
        pl.when(cond)(copy.start)
    home_a.wait()
    a_copy(a_part(b, 0), b, 0, mate)
    for copy in (home_ac, home_mc, home_rp, home_sc, home_ca):
        copy.wait()
    for d in range(1, blks):
        src = lax.rem(b + d, blks)
        remote(acol_h, ac_v.at[src], ac_send.at[d], ac_recv.at[src], (r, b)).wait_recv()
    for k in (0, 2):
        remote(mcol_h.at[t], mc_v.at[k], mc_send.at[k], mc_recv.at[k], (r, b)).wait_recv()
        remote(rpat_h.at[t], rp_v.at[k], rp_send.at[k], rp_recv.at[k], (r, b)).wait_recv()
    moves = [
        pltpu.make_async_copy(ac_v, ac_s, loc.at[2]),
        pltpu.make_async_copy(mc_v, mc_s, loc.at[3]),
        pltpu.make_async_copy(rp_v, rp_s, loc.at[4]),
    ]
    for copy in moves:
        copy.start()
    for copy in moves:
        copy.wait()

    row0 = own * x
    slots = blks * per

    def table_row(i, carry):
        pats = [rp_s[1, p, row0 + i] for p in range(q2)]
        cands = [cand_s[t, c, row0 + i] for c in range(q2)]
        for p in range(q2):
            owner = scol_s[t, pats[p]]
            diag[q2 * i + p] = jnp.where(owner == rows * r + row0 + i, 1, 0)

        def table_slot(s, inner):
            col = ac_s[s // per, s % per, row0 + i]
            present = col >= 0
            w = lax.rem(col - rows * r + reach + total, total) - row0
            w = jnp.clip(w, 0, 2 * reach + own - 1)
            rel = w + row0
            side, line = lax.shift_right_logical(rel, rows.bit_length() - 1), rel & (rows - 1)
            mc = [mc_s[side, q, line] for q in range(qm)]
            rp = [rp_s[side, q, line] for q in range(q2)]
            for p in range(q2):
                at_m, at_r = jnp.int32(zero_m), jnp.int32(zero_r)
                for q in range(qm):
                    at_m = jnp.where(present & (mc[q] == pats[p]), w * qm + q, at_m)
                for q in range(q2):
                    at_r = jnp.where(present & (rp[q] == cands[p]), w * q2 + q, at_r)
                idx_m[(i * slots + s) * q2 + p] = at_m
                idx_r[(i * slots + s) * q2 + p] = at_r
            return inner

        return lax.fori_loop(0, slots, table_slot, carry)

    lax.fori_loop(0, own, table_row, 0)

    left, right = lax.rem(x + last, chips), lax.rem(x + 1, chips)
    by_left, by_right = (r, CORES * left + t), (r, CORES * right + t)
    above, below = (up, b), (down, b)
    inner = (x >= 1) & (x <= last - 1)

    def m_rows(slot, first, count):
        return m_win.at[pl.ds(mq * slot + qm * first, qm * count)]

    def m_take(slot, h):
        part = m_rows(slot, hr * h, hr)
        remote(part, part, m_send.at[0], m_recv.at[2 * slot + h], (r, b)).wait_recv()

    relays = []
    for cond, needs, slots_of, rows_of, sem, where in (
        (x == last, ((0, 1), (0, 0)), (0, last), (1, own - 1), h_recv.at[1], by_right),
        (x == 0, ((2 * chips, 0), (2 * chips, 1)), (2 * chips, chips + 1), (0, own - 1),
         h_recv.at[1], by_left),
        (x == 1, ((2, 0),), (2, last), (0, 1), h_recv.at[0], by_left),
        (x == last - 1, ((2 * chips - 2, 1),), (2 * chips - 2, chips + 1), (own - 1, 1),
         h_recv.at[0], by_right),
        (inner, ((1, 1),), (1, 2), (hr, hr), m_recv.at[2 * 2 + 1], by_left),
        (inner, ((2 * chips - 1, 0),), (2 * chips - 1, 2 * chips - 2), (0, hr),
         m_recv.at[2 * (2 * chips - 2)], by_right),
    ):
        copy = remote(
            m_rows(slots_of[0], *rows_of), m_rows(slots_of[1], *rows_of),
            h_send.at[len(relays)], sem, where,
        )
        relays.append((cond, copy))

        def pass_on(needs=needs, copy=copy):
            for slot, h in needs:
                m_take(slot, h)
            copy.start()

        pl.when(cond)(pass_on)
    a_start(1)
    a_copy(a_part(b, 1), b, 1, mate)

    def a_swap(g):
        for d in hops:
            a_wait(chip(d), g)
            a_copy(a_part(chip(d), g), chip(d), g, mate)
        for d in range(chips):
            a_wait(CORES * across(d) + (1 - t), g)

    a_swap(0)
    home_m.wait()
    edge = (x == 0) | (x == last)
    for k in range(chips):
        for e in range(2):
            for cond, taken, slot, h in (
                (
                    k <= last - x,
                    ((x == last) & (k == 0)) | ((x == 1) & (k == 2) & (e == 1))
                    | (inner & (k == 1) & (e == 0)) | ((x == 0) & (k == last)),
                    k, 1 - e,
                ),
                (
                    k <= x,
                    ((x == 0) & (k == 0)) | ((x == last - 1) & (k == 2) & (e == 1))
                    | (inner & (k == 1) & (e == 0)) | ((x == last) & (k == last)),
                    2 * chips - k, e,
                ),
            ):
                pl.when(cond & jnp.logical_not(taken))(functools.partial(m_take, slot, h))

    def far_take(slot, one, rest):
        for k, span in ((0, (one, 1)), (1, (rest, own - 1))):
            part = m_rows(slot, *span)
            remote(part, part, h_send.at[0], h_recv.at[k], (r, b)).wait_recv()

    pl.when(x == 0)(lambda: far_take(last, 0, 1))
    pl.when(x == last)(lambda: far_take(chips + 1, own - 1, 0))

    def product(i, win, table):
        acc = None
        for k in range(blks):
            lhs = jnp.concatenate([a_win[k, i, s] for s in range(per)], axis=1)
            picks = []
            for s in range(per):
                at = (i * slots + k * per + s) * q2
                picks.append(jnp.concatenate([win[table[at + p]] for p in range(q2)], axis=1))
            rhs = jnp.concatenate(picks, axis=0)
            part = jnp.dot(lhs, rhs, preferred_element_type=jnp.float32)
            acc = part if acc is None else acc + part
        return acc

    eye = (
        lax.broadcasted_iota(jnp.int32, (n, n), 0) == lax.broadcasted_iota(jnp.int32, (n, n), 1)
    ).astype(jnp.float32)

    def resid_row(i, carry):
        summed = product(i, m_win, idx_m)
        for p in range(q2):
            block = summed[:, n * p:n * (p + 1)] - diag[q2 * i + p].astype(jnp.float32) * eye
            r_win[rq * chips + q2 * i + p] = block.astype(r_win.dtype)
            r_turn[q2 * i + p] = block.T.astype(r_turn.dtype)
        return carry

    pieces = own
    rh = rq // pieces
    r_all = []

    def piece(slot, h):
        return r_win.at[pl.ds(rq * slot + rh * h, rh)]

    def give(slot, h, to_slot, where, cond=None):
        if cond is not None:
            to_slot = jnp.clip(to_slot, 0, 2 * chips)
        copy = remote(
            piece(slot, h), piece(to_slot, h), r_send.at[len(r_all)],
            r_recv.at[pieces * to_slot + h], where,
        )
        r_all.append((cond, copy))
        if cond is None:
            copy.start()
        else:
            pl.when(cond)(copy.start)

    def take(slot, h, cond=None):
        def wait():
            remote(
                piece(slot, h), piece(slot, h), r_send.at[0], r_recv.at[pieces * slot + h], (r, b)
            ).wait_recv()

        if cond is None:
            wait()
        else:
            pl.when(cond)(wait)

    for h in range(pieces):
        if h == a_rows[1][0]:
            a_swap(1)
        resid_row(h, 0)
        give(chips, h, chips + x - right, by_right)
        give(chips, h, chips + x - left, by_left)
        give(chips, h, 0, above)
        give(chips, h, 2 * chips, below)

    at_left, at_right = chips + left - x, chips + right - x
    for h in range(pieces):
        take(at_left, h)
        if h < hr:
            give(at_left, h, chips + left - right, by_right)
        give(at_left, h, 2 * chips - 1, below, x >= 1)
        take(at_right, h)
        if h >= hr:
            give(at_right, h, chips + right - left, by_left)
        give(at_right, h, 1, above, x <= last - 1)
        take(0, h)
        give(0, h, last, by_right, x == last)
        take(2 * chips, h)
        give(2 * chips, h, chips + 1, by_left, x == 0)
    for h in range(pieces):
        take(1, h, x <= last - 1)
        give(1, h, 2, by_left, inner)
        take(2 * chips - 1, h, x >= 1)
        give(2 * chips - 1, h, 2 * chips - 2, by_right, inner)
    for h in range(pieces):
        take(jnp.where(x < 2, chips + 2, chips - 2), h)
        take(2, h, x < 2)
        take(3, h, x == 0)
        take(2 * chips - 2, h, x >= 2)
        take(chips + 1, h, x == last)

    width = n // blks
    home_o = pltpu.make_async_copy(
        r_turn.at[:, pl.ds(width * b, width), :], o_res.at[t, pl.ds(rq * x, rq)], loc.at[0]
    )
    home_o.start()
    o_out = []
    for d in range(1, blks):
        to = lax.rem(b + d, blks)
        o_out.append(remote(
            r_turn.at[:, pl.ds(width * to, width), :], o_res.at[t, pl.ds(rq * x, rq)],
            o_send.at[d], o_recv.at[b], (r, to),
        ))
        o_out[-1].start()

    def score_row(i, carry):
        proj = product(i, r_win, idx_r)
        means = jnp.sum(proj * proj, axis=0, keepdims=True) * (1.0 / n)
        for c in range(q2):
            sc_own[pl.ds(q2 * i + c, 1), :] = means[:, n * c:n * (c + 1)]
        return carry

    lax.fori_loop(0, own, score_row, 0)

    home_s = pltpu.make_async_copy(sc_own, o_sc.at[t, x], loc.at[1])
    home_s.start()
    s_out = []
    for d in (4, 3, 5, 2, 6, 7, 1):
        to = lax.rem(b + d, blks)
        s_out.append(remote(
            sc_own, o_sc.at[t, x], s_send.at[d], s_recv.at[b], (r, to)
        ))
        s_out[-1].start()

    for copy in ints + a_all + o_out + s_out:
        copy.wait_send()
    for cond, copy in m_out + relays + r_all:
        if cond is None:
            copy.wait_send()
        else:
            pl.when(cond)(copy.wait_send)
    home_o.wait()
    for d in range(1, blks):
        src = lax.rem(b + d, blks)
        sx, st = src // CORES, src % CORES
        remote(
            r_turn.at[:, pl.ds(0, width), :], o_res.at[st, pl.ds(rq * sx, rq)],
            o_send.at[d], o_recv.at[src], (r, b),
        ).wait_recv()
        remote(sc_own, o_sc.at[st, sx], s_send.at[d], s_recv.at[src], (r, b)).wait_recv()
    home_s.wait()


def on_device(rings, blks, acol, aval, mcol, mval, rpat, scol, cand):
    rows, per, n, _ = aval.shape
    slabs, _, qm = mcol.shape
    q2 = rpat.shape[2]
    chips = blks // CORES
    own = rows // chips
    window = 2 * rows + own
    dims = (rings, blks, rows, own, per, qm, q2, n)
    width = n // blks
    anywhere = pl.BlockSpec(memory_space=pl.ANY)
    dma = pltpu.SemaphoreType.DMA
    slots = blks * per
    res, sc = pl.pallas_call(
        functools.partial(kernel, dims),
        out_shape=(
            jax.ShapeDtypeStruct((slabs, rows * q2, width, n), jnp.bfloat16),
            jax.ShapeDtypeStruct((slabs, chips, own * q2, n), jnp.float32),
        ),
        in_specs=[anywhere] * 7,
        out_specs=(anywhere, anywhere),
        scratch_shapes=[
            pltpu.VMEM((blks, own, per, n, n), jnp.bfloat16),
            pltpu.VMEM((window * qm + 1, n, n), jnp.bfloat16),
            pltpu.VMEM((window * q2 + 1, n, n), jnp.bfloat16),
            pltpu.VMEM((own * q2, n, n), jnp.bfloat16),
            pltpu.VMEM((own * q2, n), jnp.float32),
            pltpu.VMEM((blks, per, rows), jnp.int32),
            pltpu.VMEM((3, qm, rows), jnp.int32),
            pltpu.VMEM((3, q2, rows), jnp.int32),
            pltpu.SMEM((blks, per, rows), jnp.int32),
            pltpu.SMEM((3, qm, rows), jnp.int32),
            pltpu.SMEM((3, q2, rows), jnp.int32),
            pltpu.SMEM(scol.shape, jnp.int32),
            pltpu.SMEM((slabs, q2, rows), jnp.int32),
            pltpu.SMEM((own * slots * q2,), jnp.int32),
            pltpu.SMEM((own * slots * q2,), jnp.int32),
            pltpu.SMEM((own * q2,), jnp.int32),
            dma((4 * chips,)), dma((2 * blks,)),
            dma((4 * chips,)), dma((4 * chips + 2,)),
            dma((11 * own,)), dma(((2 * chips + 1) * own,)),
            dma((blks,)), dma((blks,)), dma((3,)), dma((3,)), dma((3,)), dma((3,)),
            dma((blks,)), dma((blks,)), dma((blks,)), dma((blks,)),
            dma((6,)), dma((2,)), dma((7,)),
        ],
        compiler_params=pltpu.CompilerParams(
            collective_id=0, has_side_effects=True, vmem_limit_bytes=66 * 10**6
        ),
    )(
        scol, cand.swapaxes(1, 2), rpat.swapaxes(1, 2), acol.T, mcol.swapaxes(1, 2), aval,
        mval.reshape(slabs, rows * qm, n, n),
    )
    def finish(res_ref, sc_ref, o_ref, s_ref):
        b = lax.axis_index("blk")
        o_ref[...] = res_ref[...]
        for k in range(blks):

            @pl.when(b == k)
            def _():
                s_ref[...] = sc_ref[:, width * k:width * (k + 1)]

    res, sc = pl.pallas_call(
        finish,
        out_shape=(
            jax.ShapeDtypeStruct((slabs * rows * q2 * width, n), jnp.bfloat16),
            jax.ShapeDtypeStruct((slabs * rows * q2, width), jnp.float32),
        ),
    )(res.reshape(-1, n), sc.reshape(-1, n))
    resid = res.reshape(slabs, rows, q2, width, n).swapaxes(3, 4)
    return resid, sc.reshape(slabs, rows, q2, width)


def solution(mesh):
    placed = (
        P("rows", "blk"),
        P("rows", "blk", None, None),
        P(None, "rows", None),
        P(None, "rows", None, None, None),
        P(None, "rows", None),
        P(),
        P(None, "rows", None),
    )
    return jax.shard_map(
        functools.partial(on_device, mesh.shape["rows"], mesh.shape["blk"]),
        mesh=mesh,
        in_specs=placed,
        out_specs=(P(None, "rows", None, None, "blk"), P(None, "rows", None, "blk")),
        check_vma=False,
    )
```

```python
import functools

import jax
import jax.numpy as jnp
from jax import lax
from jax.experimental import pallas as pl
from jax.experimental.pallas import tpu as pltpu
from jax.sharding import PartitionSpec as P

MESH = pl.DeviceIdType.MESH
CORES = 2


def kernel(
    dims,
    scol_h, cand_h, rpat_h, acol_h, mcol_h, aval_h, mval_h,
    o_res, o_sc,
    a_win, m_win, r_win, r_turn, sc_own, ac_v, mc_v, rp_v,
    ac_s, mc_s, rp_s, scol_s, cand_s, idx_m, idx_r, diag,
    a_send, a_recv, m_send, m_recv, r_send, r_recv,
    ac_send, ac_recv, mc_send, mc_recv, rp_send, rp_recv,
    o_send, o_recv, s_send, s_recv, h_send, h_recv, loc,
):
    rings, blks, rows, own, per, qm, q2, n = dims
    chips = blks // CORES
    reach = rows
    total = rings * rows
    r, b = lax.axis_index("rows"), lax.axis_index("blk")
    x, t = b // CORES, b % CORES
    up, down = lax.rem(r + 1, rings), lax.rem(r + rings - 1, rings)
    mate = (r, CORES * x + (1 - t))
    mq, rq = own * qm, own * q2
    zero_m, zero_r = m_win.shape[0] - 1, r_win.shape[0] - 1

    def remote(src, dst, send, recv, where):
        return pltpu.make_async_remote_copy(
            src_ref=src, dst_ref=dst, send_sem=send, recv_sem=recv,
            device_id=where, device_id_type=MESH,
        )

    def across(d):
        return lax.rem(x + d, chips)

    def chip(d):
        return CORES * across(d) + t

    home_a = pltpu.make_async_copy(aval_h.at[pl.ds(own * x, own)], a_win.at[b], loc.at[0])
    home_m = pltpu.make_async_copy(
        mval_h.at[t], m_win.at[pl.ds(mq * (chips - x), mq * chips)], loc.at[1]
    )
    home_ac = pltpu.make_async_copy(acol_h, ac_v.at[b], loc.at[2])
    home_mc = pltpu.make_async_copy(mcol_h.at[t], mc_v.at[1], loc.at[3])
    home_rp = pltpu.make_async_copy(rpat_h.at[t], rp_v.at[1], loc.at[4])
    home_sc = pltpu.make_async_copy(scol_h, scol_s, loc.at[5])
    home_ca = pltpu.make_async_copy(cand_h, cand_s, loc.at[6])

    barrier = pltpu.get_barrier_semaphore()
    for ring in (up, down):
        pl.semaphore_signal(barrier, inc=1, device_id=(ring, b), device_id_type=MESH)
    for d in range(1, blks):
        pl.semaphore_signal(
            barrier, inc=1, device_id=(r, lax.rem(b + d, blks)), device_id_type=MESH
        )
    left, right = lax.rem(x + chips - 1, chips), lax.rem(x + 1, chips)
    for ring, side in ((up, left), (down, right)):
        pl.semaphore_signal(
            barrier, inc=1, device_id=(ring, CORES * side + t), device_id_type=MESH
        )
    for copy in (home_ac, home_mc, home_rp, home_sc, home_ca, home_a, home_m):
        copy.start()
    m_win[zero_m] = jnp.zeros((n, n), m_win.dtype)
    r_win[zero_r] = jnp.zeros((n, n), r_win.dtype)
    pl.semaphore_wait(barrier, blks - 1 + 4)

    hr = own // 2
    hops = (1, chips - 1) + tuple(range(2, chips - 1))
    a_all = []
    a_rows = ((0, own - 1), (own - 1, 1))

    def a_part(src, g):
        return a_win.at[src, pl.ds(*a_rows[g])]

    def a_copy(source, src, g, where):
        copy = remote(
            source, a_part(src, g), a_send.at[len(a_all)], a_recv.at[blks * g + src], where
        )
        copy.start()
        a_all.append(copy)

    def a_wait(src, g):
        remote(
            a_part(src, g), a_part(src, g), a_send.at[0], a_recv.at[blks * g + src], (r, b)
        ).wait_recv()

    ints = []
    for d in range(1, blks):
        to = lax.rem(b + d, blks)
        ints.append(remote(acol_h, ac_v.at[b], ac_send.at[d], ac_recv.at[b], (r, to)))
    for k, ring in ((0, up), (2, down)):
        ints.append(remote(mcol_h.at[t], mc_v.at[k], mc_send.at[k], mc_recv.at[k], (ring, b)))
        ints.append(remote(rpat_h.at[t], rp_v.at[k], rp_send.at[k], rp_recv.at[k], (ring, b)))
    for copy in ints:
        copy.start()


    def a_start(g):
        for d in hops:
            a_copy(aval_h.at[pl.ds(own * across(d) + a_rows[g][0], a_rows[g][1])], b, g, (r, chip(d)))

    a_start(0)
    last = chips - 1
    m_out = []
    mh = mq // 2
    for k in range(chips):
        for e in range(2):
            for cond, skip, j, h, slot, ring in (
                (x <= last - k, ((1, 0), (0, 0), (0, 1), (0, 2)), last - k, 1 - e, last - k - x, up),
                (x >= k, ((last - 1, 0), (last, 0), (last, 1), (last, 2)), k, e,
                 2 * chips + k - x, down),
            ):
                if k == 0 and e == 0:
                    cond &= (x != skip[0][0]) & (x != skip[1][0])
                elif k == 0 or (k == 1 and e == 0):
                    cond &= x != skip[1][0]
                safe = jnp.clip(slot, 0, 2 * chips)
                m_out.append((cond, remote(
                    mval_h.at[t, pl.ds(mq * j + mh * h, mh)],
                    m_win.at[pl.ds(mq * safe + mh * h, mh)],
                    m_send.at[len(m_out)], m_recv.at[2 * safe + h], (ring, b),
                )))
    for cond, copy in m_out:
        pl.when(cond)(copy.start)
    home_a.wait()
    a_copy(a_part(b, 0), b, 0, mate)
    for copy in (home_ac, home_mc, home_rp, home_sc, home_ca):
        copy.wait()
    for d in range(1, blks):
        src = lax.rem(b + d, blks)
        remote(acol_h, ac_v.at[src], ac_send.at[d], ac_recv.at[src], (r, b)).wait_recv()
    for k in (0, 2):
        remote(mcol_h.at[t], mc_v.at[k], mc_send.at[k], mc_recv.at[k], (r, b)).wait_recv()
        remote(rpat_h.at[t], rp_v.at[k], rp_send.at[k], rp_recv.at[k], (r, b)).wait_recv()
    moves = [
        pltpu.make_async_copy(ac_v, ac_s, loc.at[2]),
        pltpu.make_async_copy(mc_v, mc_s, loc.at[3]),
        pltpu.make_async_copy(rp_v, rp_s, loc.at[4]),
    ]
    for copy in moves:
        copy.start()
    for copy in moves:
        copy.wait()

    row0 = own * x
    slots = blks * per

    def table_row(i, carry):
        pats = [rp_s[1, p, row0 + i] for p in range(q2)]
        cands = [cand_s[t, c, row0 + i] for c in range(q2)]
        for p in range(q2):
            owner = scol_s[t, pats[p]]
            diag[q2 * i + p] = jnp.where(owner == rows * r + row0 + i, 1, 0)

        def table_slot(s, inner):
            col = ac_s[s // per, s % per, row0 + i]
            present = col >= 0
            w = lax.rem(col - rows * r + reach + total, total) - row0
            w = jnp.clip(w, 0, 2 * reach + own - 1)
            rel = w + row0
            side, line = lax.shift_right_logical(rel, rows.bit_length() - 1), rel & (rows - 1)
            mc = [mc_s[side, q, line] for q in range(qm)]
            rp = [rp_s[side, q, line] for q in range(q2)]
            for p in range(q2):
                at_m, at_r = jnp.int32(zero_m), jnp.int32(zero_r)
                for q in range(qm):
                    at_m = jnp.where(present & (mc[q] == pats[p]), w * qm + q, at_m)
                for q in range(q2):
                    at_r = jnp.where(present & (rp[q] == cands[p]), w * q2 + q, at_r)
                idx_m[(i * slots + s) * q2 + p] = at_m
                idx_r[(i * slots + s) * q2 + p] = at_r
            return inner

        return lax.fori_loop(0, slots, table_slot, carry)

    lax.fori_loop(0, own, table_row, 0)

    by_left, by_right = (r, CORES * left + t), (r, CORES * right + t)
    above, below = (up, b), (down, b)
    inner = (x >= 1) & (x <= last - 1)

    def m_rows(slot, first, count):
        return m_win.at[pl.ds(mq * slot + qm * first, qm * count)]

    def m_take(slot, h):
        part = m_rows(slot, hr * h, hr)
        remote(part, part, m_send.at[0], m_recv.at[2 * slot + h], (r, b)).wait_recv()

    relays = []
    for cond, needs, slots_of, rows_of, sem, where in (
        (x == last, ((0, 1), (0, 0)), (0, last), (1, own - 1), h_recv.at[1], by_right),
        (x == 0, ((2 * chips, 0), (2 * chips, 1)), (2 * chips, chips + 1), (0, own - 1),
         h_recv.at[1], by_left),
        (x == 1, ((2, 0),), (2, last), (0, 1), h_recv.at[0], by_left),
        (x == last - 1, ((2 * chips - 2, 1),), (2 * chips - 2, chips + 1), (own - 1, 1),
         h_recv.at[0], by_right),
        (inner, ((1, 1),), (1, 2), (hr, hr), m_recv.at[2 * 2 + 1], by_left),
        (inner, ((2 * chips - 1, 0),), (2 * chips - 1, 2 * chips - 2), (0, hr),
         m_recv.at[2 * (2 * chips - 2)], by_right),
    ):
        copy = remote(
            m_rows(slots_of[0], *rows_of), m_rows(slots_of[1], *rows_of),
            h_send.at[len(relays)], sem, where,
        )
        relays.append((cond, copy))

        def pass_on(needs=needs, copy=copy):
            for slot, h in needs:
                m_take(slot, h)
            copy.start()

        pl.when(cond)(pass_on)
    a_start(1)
    a_copy(a_part(b, 1), b, 1, mate)

    def a_swap(g):
        for d in hops:
            a_wait(chip(d), g)
            a_copy(a_part(chip(d), g), chip(d), g, mate)
        for d in range(chips):
            a_wait(CORES * across(d) + (1 - t), g)

    a_swap(0)
    home_m.wait()
    edge = (x == 0) | (x == last)
    for k in range(chips):
        for e in range(2):
            for cond, taken, slot, h in (
                (
                    k <= last - x,
                    ((x == last) & (k == 0)) | ((x == 1) & (k == 2) & (e == 1))
                    | (inner & (k == 1) & (e == 0)) | ((x == 0) & (k == last)),
                    k, 1 - e,
                ),
                (
                    k <= x,
                    ((x == 0) & (k == 0)) | ((x == last - 1) & (k == 2) & (e == 1))
                    | (inner & (k == 1) & (e == 0)) | ((x == last) & (k == last)),
                    2 * chips - k, e,
                ),
            ):
                pl.when(cond & jnp.logical_not(taken))(functools.partial(m_take, slot, h))

    def far_take(slot, one, rest):
        for k, span in ((0, (one, 1)), (1, (rest, own - 1))):
            part = m_rows(slot, *span)
            remote(part, part, h_send.at[0], h_recv.at[k], (r, b)).wait_recv()

    pl.when(x == 0)(lambda: far_take(last, 0, 1))
    pl.when(x == last)(lambda: far_take(chips + 1, own - 1, 0))

    def product(i, win, table):
        acc = None
        for k in range(blks):
            lhs = jnp.concatenate([a_win[k, i, s] for s in range(per)], axis=1)
            picks = []
            for s in range(per):
                at = (i * slots + k * per + s) * q2
                picks.append(jnp.concatenate([win[table[at + p]] for p in range(q2)], axis=1))
            rhs = jnp.concatenate(picks, axis=0)
            part = jnp.dot(lhs, rhs, preferred_element_type=jnp.float32)
            acc = part if acc is None else acc + part
        return acc

    eye = (
        lax.broadcasted_iota(jnp.int32, (n, n), 0) == lax.broadcasted_iota(jnp.int32, (n, n), 1)
    ).astype(jnp.float32)

    def resid_row(i, carry):
        summed = product(i, m_win, idx_m)
        for p in range(q2):
            block = summed[:, n * p:n * (p + 1)] - diag[q2 * i + p].astype(jnp.float32) * eye
            r_win[rq * chips + q2 * i + p] = block.astype(r_win.dtype)
        return carry

    pieces, direct = own, own - 1
    rh = rq // pieces
    r_all = []

    def piece(slot, h):
        return r_win.at[pl.ds(rq * slot + rh * h, rh)]

    def give(slot, h, to_slot, where, cond=None):
        if cond is not None:
            to_slot = jnp.clip(to_slot, 0, 2 * chips)
        copy = remote(
            piece(slot, h), piece(to_slot, h), r_send.at[len(r_all)],
            r_recv.at[pieces * to_slot + h], where,
        )
        r_all.append((cond, copy))
        if cond is None:
            copy.start()
        else:
            pl.when(cond)(copy.start)

    def take(slot, h, cond=None):
        def wait():
            remote(
                piece(slot, h), piece(slot, h), r_send.at[0], r_recv.at[pieces * slot + h], (r, b)
            ).wait_recv()

        if cond is None:
            wait()
        else:
            pl.when(cond)(wait)

    for h in range(pieces):
        if h == a_rows[1][0]:
            a_swap(1)
        resid_row(h, 0)
        give(chips, h, chips + x - right, by_right)
        give(chips, h, chips + x - left, by_left)
        give(chips, h, 0, above)
        give(chips, h, 2 * chips, below)

    for k in range(rq):
        block = r_win[rq * chips + k].astype(jnp.float32)
        r_turn[k] = block.T.astype(r_turn.dtype)

    at_left, at_right = chips + left - x, chips + right - x
    for h in range(pieces):
        take(at_left, h)
        if h < hr:
            give(at_left, h, chips + left - right, by_right)
        give(at_left, h, 2 * chips - 1, below, x >= 1)
        if h >= direct:
            give(at_left, h, 2 * chips - 2, (down, CORES * right + t), inner)
        take(at_right, h)
        if h >= hr:
            give(at_right, h, chips + right - left, by_left)
        give(at_right, h, 1, above, x <= last - 1)
        if h >= direct:
            give(at_right, h, 2, (up, CORES * left + t), inner)
        if h >= direct:
            give(at_left, h, last, above, x == 0)
            give(at_right, h, chips + 1, below, x == last)
        take(0, h)
        if h < direct:
            give(0, h, last, by_right, x == last)
        take(2 * chips, h)
        if h < direct:
            give(2 * chips, h, chips + 1, by_left, x == 0)
    for h in range(pieces):
        take(1, h, x <= last - 1)
        if h < direct:
            give(1, h, 2, by_left, inner)
        take(2 * chips - 1, h, x >= 1)
        if h < direct:
            give(2 * chips - 1, h, 2 * chips - 2, by_right, inner)
    for h in range(pieces):
        take(jnp.where(x < 2, chips + 2, chips - 2), h)
        take(2, h, x < 2)
        take(3, h, x == 0)
        take(2 * chips - 2, h, x >= 2)
        take(chips + 1, h, x == last)

    width = n // blks
    home_o = pltpu.make_async_copy(
        r_turn.at[:, pl.ds(width * b, width), :], o_res.at[t, pl.ds(rq * x, rq)], loc.at[0]
    )
    home_o.start()
    o_out = []
    for d in range(1, blks):
        to = lax.rem(b + d, blks)
        o_out.append(remote(
            r_turn.at[:, pl.ds(width * to, width), :], o_res.at[t, pl.ds(rq * x, rq)],
            o_send.at[d], o_recv.at[b], (r, to),
        ))
        o_out[-1].start()

    def score_row(i, carry):
        proj = product(i, r_win, idx_r)
        means = jnp.sum(proj * proj, axis=0, keepdims=True) * (1.0 / n)
        for c in range(q2):
            sc_own[pl.ds(q2 * i + c, 1), :] = means[:, n * c:n * (c + 1)]
        return carry

    lax.fori_loop(0, own, score_row, 0)

    home_s = pltpu.make_async_copy(sc_own, o_sc.at[t, x], loc.at[1])
    home_s.start()
    s_out = []
    for d in (4, 3, 5, 2, 6, 7, 1):
        to = lax.rem(b + d, blks)
        s_out.append(remote(
            sc_own, o_sc.at[t, x], s_send.at[d], s_recv.at[b], (r, to)
        ))
        s_out[-1].start()

    for copy in ints + a_all + o_out + s_out:
        copy.wait_send()
    for cond, copy in m_out + relays + r_all:
        if cond is None:
            copy.wait_send()
        else:
            pl.when(cond)(copy.wait_send)
    home_o.wait()
    for d in range(1, blks):
        src = lax.rem(b + d, blks)
        sx, st = src // CORES, src % CORES
        remote(
            r_turn.at[:, pl.ds(0, width), :], o_res.at[st, pl.ds(rq * sx, rq)],
            o_send.at[d], o_recv.at[src], (r, b),
        ).wait_recv()
        remote(sc_own, o_sc.at[st, sx], s_send.at[d], s_recv.at[src], (r, b)).wait_recv()
    home_s.wait()


def on_device(rings, blks, acol, aval, mcol, mval, rpat, scol, cand):
    rows, per, n, _ = aval.shape
    slabs, _, qm = mcol.shape
    q2 = rpat.shape[2]
    chips = blks // CORES
    own = rows // chips
    window = 2 * rows + own
    dims = (rings, blks, rows, own, per, qm, q2, n)
    width = n // blks
    anywhere = pl.BlockSpec(memory_space=pl.ANY)
    dma = pltpu.SemaphoreType.DMA
    slots = blks * per
    res, sc = pl.pallas_call(
        functools.partial(kernel, dims),
        out_shape=(
            jax.ShapeDtypeStruct((slabs, rows * q2, width, n), jnp.bfloat16),
            jax.ShapeDtypeStruct((slabs, chips, own * q2, n), jnp.float32),
        ),
        in_specs=[anywhere] * 7,
        out_specs=(anywhere, anywhere),
        scratch_shapes=[
            pltpu.VMEM((blks, own, per, n, n), jnp.bfloat16),
            pltpu.VMEM((window * qm + 1, n, n), jnp.bfloat16),
            pltpu.VMEM((window * q2 + 1, n, n), jnp.bfloat16),
            pltpu.VMEM((own * q2, n, n), jnp.bfloat16),
            pltpu.VMEM((own * q2, n), jnp.float32),
            pltpu.VMEM((blks, per, rows), jnp.int32),
            pltpu.VMEM((3, qm, rows), jnp.int32),
            pltpu.VMEM((3, q2, rows), jnp.int32),
            pltpu.SMEM((blks, per, rows), jnp.int32),
            pltpu.SMEM((3, qm, rows), jnp.int32),
            pltpu.SMEM((3, q2, rows), jnp.int32),
            pltpu.SMEM(scol.shape, jnp.int32),
            pltpu.SMEM((slabs, q2, rows), jnp.int32),
            pltpu.SMEM((own * slots * q2,), jnp.int32),
            pltpu.SMEM((own * slots * q2,), jnp.int32),
            pltpu.SMEM((own * q2,), jnp.int32),
            dma((4 * chips,)), dma((2 * blks,)),
            dma((4 * chips,)), dma((4 * chips + 2,)),
            dma((11 * own,)), dma(((2 * chips + 1) * own,)),
            dma((blks,)), dma((blks,)), dma((3,)), dma((3,)), dma((3,)), dma((3,)),
            dma((blks,)), dma((blks,)), dma((blks,)), dma((blks,)),
            dma((6,)), dma((2,)), dma((7,)),
        ],
        compiler_params=pltpu.CompilerParams(
            collective_id=0, has_side_effects=True, vmem_limit_bytes=66 * 10**6
        ),
    )(
        scol, cand.swapaxes(1, 2), rpat.swapaxes(1, 2), acol.T, mcol.swapaxes(1, 2), aval,
        mval.reshape(slabs, rows * qm, n, n),
    )
    def finish(res_ref, sc_ref, o_ref, s_ref):
        b = lax.axis_index("blk")
        o_ref[...] = res_ref[...]
        for k in range(blks):

            @pl.when(b == k)
            def _():
                s_ref[...] = sc_ref[:, width * k:width * (k + 1)]

    res, sc = pl.pallas_call(
        finish,
        out_shape=(
            jax.ShapeDtypeStruct((slabs * rows * q2 * width, n), jnp.bfloat16),
            jax.ShapeDtypeStruct((slabs * rows * q2, width), jnp.float32),
        ),
    )(res.reshape(-1, n), sc.reshape(-1, n))
    resid = res.reshape(slabs, rows, q2, width, n).swapaxes(3, 4)
    return resid, sc.reshape(slabs, rows, q2, width)


def solution(mesh):
    placed = (
        P("rows", "blk"),
        P("rows", "blk", None, None),
        P(None, "rows", None),
        P(None, "rows", None, None, None),
        P(None, "rows", None),
        P(),
        P(None, "rows", None),
    )
    return jax.shard_map(
        functools.partial(on_device, mesh.shape["rows"], mesh.shape["blk"]),
        mesh=mesh,
        in_specs=placed,
        out_specs=(P(None, "rows", None, None, "blk"), P(None, "rows", None, "blk")),
        check_vma=False,
    )
```

```python
import functools

import jax
import jax.numpy as jnp
from jax import lax
from jax.experimental import pallas as pl
from jax.experimental.pallas import tpu as pltpu
from jax.sharding import PartitionSpec as P

MESH = pl.DeviceIdType.MESH
CORES = 2


def kernel(
    dims,
    scol_h, cand_h, rpat_h, acol_h, mcol_h, aval_h, mval_h,
    o_res, o_sc,
    a_win, m_win, r_win, r_turn, sc_own, ac_v, mc_v, rp_v,
    ac_s, mc_s, rp_s, scol_s, cand_s, idx_m, idx_r, diag,
    a_send, a_recv, m_send, m_recv, r_send, r_recv,
    ac_send, ac_recv, mc_send, mc_recv, rp_send, rp_recv,
    o_send, o_recv, s_send, s_recv, h_send, h_recv, loc,
):
    rings, blks, rows, own, per, qm, q2, n = dims
    chips = blks // CORES
    reach = rows
    total = rings * rows
    r, b = lax.axis_index("rows"), lax.axis_index("blk")
    x, t = b // CORES, b % CORES
    up, down = lax.rem(r + 1, rings), lax.rem(r + rings - 1, rings)
    mate = (r, CORES * x + (1 - t))
    mq, rq = own * qm, own * q2
    zero_m, zero_r = m_win.shape[0] - 1, r_win.shape[0] - 1

    def remote(src, dst, send, recv, where):
        return pltpu.make_async_remote_copy(
            src_ref=src, dst_ref=dst, send_sem=send, recv_sem=recv,
            device_id=where, device_id_type=MESH,
        )

    def across(d):
        return lax.rem(x + d, chips)

    def chip(d):
        return CORES * across(d) + t

    home_a = pltpu.make_async_copy(aval_h.at[pl.ds(own * x, own)], a_win.at[b], loc.at[0])
    home_m = pltpu.make_async_copy(
        mval_h.at[t], m_win.at[pl.ds(mq * (chips - x), mq * chips)], loc.at[1]
    )
    home_ac = pltpu.make_async_copy(acol_h, ac_v.at[b], loc.at[2])
    home_mc = pltpu.make_async_copy(mcol_h.at[t], mc_v.at[1], loc.at[3])
    home_rp = pltpu.make_async_copy(rpat_h.at[t], rp_v.at[1], loc.at[4])
    home_sc = pltpu.make_async_copy(scol_h, scol_s, loc.at[5])
    home_ca = pltpu.make_async_copy(cand_h, cand_s, loc.at[6])

    barrier = pltpu.get_barrier_semaphore()
    for ring in (up, down):
        pl.semaphore_signal(barrier, inc=1, device_id=(ring, b), device_id_type=MESH)
    for d in range(1, blks):
        pl.semaphore_signal(
            barrier, inc=1, device_id=(r, lax.rem(b + d, blks)), device_id_type=MESH
        )
    left, right = lax.rem(x + chips - 1, chips), lax.rem(x + 1, chips)
    for ring, side in ((up, left), (down, right)):
        pl.semaphore_signal(
            barrier, inc=1, device_id=(ring, CORES * side + t), device_id_type=MESH
        )
    for copy in (home_ac, home_mc, home_rp, home_sc, home_ca, home_a, home_m):
        copy.start()
    m_win[zero_m] = jnp.zeros((n, n), m_win.dtype)
    r_win[zero_r] = jnp.zeros((n, n), r_win.dtype)
    pl.semaphore_wait(barrier, blks - 1 + 4)

    hr = own // 2
    hops = (1, chips - 1) + tuple(range(2, chips - 1))
    a_all = []
    a_rows = ((0, own - 1), (own - 1, 1))

    def a_part(src, g):
        return a_win.at[src, pl.ds(*a_rows[g])]

    def a_copy(source, src, g, where):
        copy = remote(
            source, a_part(src, g), a_send.at[len(a_all)], a_recv.at[blks * g + src], where
        )
        copy.start()
        a_all.append(copy)

    def a_wait(src, g):
        remote(
            a_part(src, g), a_part(src, g), a_send.at[0], a_recv.at[blks * g + src], (r, b)
        ).wait_recv()

    ints = []
    for d in range(1, blks):
        to = lax.rem(b + d, blks)
        ints.append(remote(acol_h, ac_v.at[b], ac_send.at[d], ac_recv.at[b], (r, to)))
    for k, ring in ((0, up), (2, down)):
        ints.append(remote(mcol_h.at[t], mc_v.at[k], mc_send.at[k], mc_recv.at[k], (ring, b)))
        ints.append(remote(rpat_h.at[t], rp_v.at[k], rp_send.at[k], rp_recv.at[k], (ring, b)))
    for copy in ints:
        copy.start()


    def a_start(g):
        for d in hops:
            a_copy(aval_h.at[pl.ds(own * across(d) + a_rows[g][0], a_rows[g][1])], b, g, (r, chip(d)))

    a_start(0)
    last = chips - 1
    m_out = []
    mh = mq // 2
    for k in range(chips):
        for e in range(2):
            for cond, skip, j, h, slot, ring in (
                (x <= last - k, ((1, 0), (0, 0), (0, 1), (0, 2)), last - k, 1 - e, last - k - x, up),
                (x >= k, ((last - 1, 0), (last, 0), (last, 1), (last, 2)), k, e,
                 2 * chips + k - x, down),
            ):
                if k == 0 and e == 0:
                    cond &= (x != skip[0][0]) & (x != skip[1][0])
                elif k == 0 or (k == 1 and e == 0):
                    cond &= x != skip[1][0]
                safe = jnp.clip(slot, 0, 2 * chips)
                m_out.append((cond, remote(
                    mval_h.at[t, pl.ds(mq * j + mh * h, mh)],
                    m_win.at[pl.ds(mq * safe + mh * h, mh)],
                    m_send.at[len(m_out)], m_recv.at[2 * safe + h], (ring, b),
                )))
    for cond, copy in m_out:
        pl.when(cond)(copy.start)
    home_a.wait()
    a_copy(a_part(b, 0), b, 0, mate)
    for copy in (home_ac, home_mc, home_rp, home_sc, home_ca):
        copy.wait()
    for d in range(1, blks):
        src = lax.rem(b + d, blks)
        remote(acol_h, ac_v.at[src], ac_send.at[d], ac_recv.at[src], (r, b)).wait_recv()
    for k in (0, 2):
        remote(mcol_h.at[t], mc_v.at[k], mc_send.at[k], mc_recv.at[k], (r, b)).wait_recv()
        remote(rpat_h.at[t], rp_v.at[k], rp_send.at[k], rp_recv.at[k], (r, b)).wait_recv()
    moves = [
        pltpu.make_async_copy(ac_v, ac_s, loc.at[2]),
        pltpu.make_async_copy(mc_v, mc_s, loc.at[3]),
        pltpu.make_async_copy(rp_v, rp_s, loc.at[4]),
    ]
    for copy in moves:
        copy.start()
    for copy in moves:
        copy.wait()

    row0 = own * x
    slots = blks * per

    def table_row(i, carry):
        pats = [rp_s[1, p, row0 + i] for p in range(q2)]
        cands = [cand_s[t, c, row0 + i] for c in range(q2)]
        for p in range(q2):
            owner = scol_s[t, pats[p]]
            diag[q2 * i + p] = jnp.where(owner == rows * r + row0 + i, 1, 0)

        def table_slot(s, inner):
            col = ac_s[s // per, s % per, row0 + i]
            present = col >= 0
            w = lax.rem(col - rows * r + reach + total, total) - row0
            w = jnp.clip(w, 0, 2 * reach + own - 1)
            rel = w + row0
            side, line = lax.shift_right_logical(rel, rows.bit_length() - 1), rel & (rows - 1)
            mc = [mc_s[side, q, line] for q in range(qm)]
            rp = [rp_s[side, q, line] for q in range(q2)]
            for p in range(q2):
                at_m, at_r = jnp.int32(zero_m), jnp.int32(zero_r)
                for q in range(qm):
                    at_m = jnp.where(present & (mc[q] == pats[p]), w * qm + q, at_m)
                for q in range(q2):
                    at_r = jnp.where(present & (rp[q] == cands[p]), w * q2 + q, at_r)
                idx_m[(i * slots + s) * q2 + p] = at_m
                idx_r[(i * slots + s) * q2 + p] = at_r
            return inner

        return lax.fori_loop(0, slots, table_slot, carry)

    lax.fori_loop(0, own, table_row, 0)

    by_left, by_right = (r, CORES * left + t), (r, CORES * right + t)
    above, below = (up, b), (down, b)
    inner = (x >= 1) & (x <= last - 1)

    def m_rows(slot, first, count):
        return m_win.at[pl.ds(mq * slot + qm * first, qm * count)]

    def m_take(slot, h):
        part = m_rows(slot, hr * h, hr)
        remote(part, part, m_send.at[0], m_recv.at[2 * slot + h], (r, b)).wait_recv()

    relays = []
    for cond, needs, slots_of, rows_of, sem, where in (
        (x == last, ((0, 1), (0, 0)), (0, last), (1, own - 1), h_recv.at[1], by_right),
        (x == 0, ((2 * chips, 0), (2 * chips, 1)), (2 * chips, chips + 1), (0, own - 1),
         h_recv.at[1], by_left),
        (x == 1, ((2, 0),), (2, last), (0, 1), h_recv.at[0], by_left),
        (x == last - 1, ((2 * chips - 2, 1),), (2 * chips - 2, chips + 1), (own - 1, 1),
         h_recv.at[0], by_right),
        (inner, ((1, 1),), (1, 2), (hr, hr), m_recv.at[2 * 2 + 1], by_left),
        (inner, ((2 * chips - 1, 0),), (2 * chips - 1, 2 * chips - 2), (0, hr),
         m_recv.at[2 * (2 * chips - 2)], by_right),
    ):
        copy = remote(
            m_rows(slots_of[0], *rows_of), m_rows(slots_of[1], *rows_of),
            h_send.at[len(relays)], sem, where,
        )
        relays.append((cond, copy))

        def pass_on(needs=needs, copy=copy):
            for slot, h in needs:
                m_take(slot, h)
            copy.start()

        pl.when(cond)(pass_on)
    a_start(1)
    a_copy(a_part(b, 1), b, 1, mate)

    def a_swap(g):
        for d in hops:
            a_wait(chip(d), g)
            a_copy(a_part(chip(d), g), chip(d), g, mate)
        for d in range(chips):
            a_wait(CORES * across(d) + (1 - t), g)

    a_swap(0)
    home_m.wait()
    edge = (x == 0) | (x == last)
    for k in range(chips):
        for e in range(2):
            for cond, taken, slot, h in (
                (
                    k <= last - x,
                    ((x == last) & (k == 0)) | ((x == 1) & (k == 2) & (e == 1))
                    | (inner & (k == 1) & (e == 0)) | ((x == 0) & (k == last)),
                    k, 1 - e,
                ),
                (
                    k <= x,
                    ((x == 0) & (k == 0)) | ((x == last - 1) & (k == 2) & (e == 1))
                    | (inner & (k == 1) & (e == 0)) | ((x == last) & (k == last)),
                    2 * chips - k, e,
                ),
            ):
                pl.when(cond & jnp.logical_not(taken))(functools.partial(m_take, slot, h))

    def far_take(slot, one, rest):
        for k, span in ((0, (one, 1)), (1, (rest, own - 1))):
            part = m_rows(slot, *span)
            remote(part, part, h_send.at[0], h_recv.at[k], (r, b)).wait_recv()

    pl.when(x == 0)(lambda: far_take(last, 0, 1))
    pl.when(x == last)(lambda: far_take(chips + 1, own - 1, 0))

    def product(i, win, table):
        acc = None
        for k in range(blks):
            lhs = jnp.concatenate([a_win[k, i, s] for s in range(per)], axis=1)
            picks = []
            for s in range(per):
                at = (i * slots + k * per + s) * q2
                picks.append(jnp.concatenate([win[table[at + p]] for p in range(q2)], axis=1))
            rhs = jnp.concatenate(picks, axis=0)
            part = jnp.dot(lhs, rhs, preferred_element_type=jnp.float32)
            acc = part if acc is None else acc + part
        return acc

    eye = (
        lax.broadcasted_iota(jnp.int32, (n, n), 0) == lax.broadcasted_iota(jnp.int32, (n, n), 1)
    ).astype(jnp.float32)

    def resid_row(i, carry):
        summed = product(i, m_win, idx_m)
        for p in range(q2):
            block = summed[:, n * p:n * (p + 1)] - diag[q2 * i + p].astype(jnp.float32) * eye
            r_win[rq * chips + q2 * i + p] = block.astype(r_win.dtype)
        return carry

    pieces, direct = own, own - 1
    rh = rq // pieces
    r_all = []

    def piece(slot, h):
        return r_win.at[pl.ds(rq * slot + rh * h, rh)]

    def give(slot, h, to_slot, where, cond=None):
        if cond is not None:
            to_slot = jnp.clip(to_slot, 0, 2 * chips)
        copy = remote(
            piece(slot, h), piece(to_slot, h), r_send.at[len(r_all)],
            r_recv.at[pieces * to_slot + h], where,
        )
        r_all.append((cond, copy))
        if cond is None:
            copy.start()
        else:
            pl.when(cond)(copy.start)

    def take(slot, h, cond=None):
        def wait():
            remote(
                piece(slot, h), piece(slot, h), r_send.at[0], r_recv.at[pieces * slot + h], (r, b)
            ).wait_recv()

        if cond is None:
            wait()
        else:
            pl.when(cond)(wait)

    for h in range(pieces):
        if h == a_rows[1][0]:
            a_swap(1)
        resid_row(h, 0)
        give(chips, h, chips + x - right, by_right)
        give(chips, h, chips + x - left, by_left)
        give(chips, h, 0, above)
        give(chips, h, 2 * chips, below)

    for k in range(rq):
        block = r_win[rq * chips + k].astype(jnp.float32)
        r_turn[k] = block.T.astype(r_turn.dtype)

    at_left, at_right = chips + left - x, chips + right - x
    for h in range(pieces):
        take(at_left, h)
        if h < hr:
            give(at_left, h, chips + left - right, by_right)
        give(at_left, h, 2 * chips - 1, below, x >= 1)
        if h >= direct:
            give(at_left, h, 2 * chips - 2, (down, CORES * right + t), inner)
        take(at_right, h)
        if h >= hr:
            give(at_right, h, chips + right - left, by_left)
        give(at_right, h, 1, above, x <= last - 1)
        if h >= direct:
            give(at_right, h, 2, (up, CORES * left + t), inner)
        if h >= direct:
            give(at_left, h, last, above, x == 0)
            give(at_right, h, chips + 1, below, x == last)
        if h < direct:
            take(0, h, x == last)
            give(0, h, last, by_right, x == last)
            take(2 * chips, h, x == 0)
            give(2 * chips, h, chips + 1, by_left, x == 0)
    for h in range(pieces):
        take(1, h, x <= last - 1)
        if h < direct:
            give(1, h, 2, by_left, inner)
        take(2 * chips - 1, h, x >= 1)
        if h < direct:
            give(2 * chips - 1, h, 2 * chips - 2, by_right, inner)
    for h in range(pieces):
        take(0, h, None if h == direct else x != last)
        take(2 * chips, h, None if h == direct else x != 0)
        take(jnp.where(x < 2, chips + 2, chips - 2), h)
        take(2, h, x < 2)
        take(3, h, x == 0)
        take(2 * chips - 2, h, x >= 2)
        take(chips + 1, h, x == last)

    width = n // blks
    home_o = pltpu.make_async_copy(
        r_turn.at[:, pl.ds(width * b, width), :], o_res.at[t, pl.ds(rq * x, rq)], loc.at[0]
    )
    home_o.start()
    o_out = []
    for d in range(1, blks):
        to = lax.rem(b + d, blks)
        o_out.append(remote(
            r_turn.at[:, pl.ds(width * to, width), :], o_res.at[t, pl.ds(rq * x, rq)],
            o_send.at[d], o_recv.at[b], (r, to),
        ))
        o_out[-1].start()

    def score_row(i, carry):
        proj = product(i, r_win, idx_r)
        means = jnp.sum(proj * proj, axis=0, keepdims=True) * (1.0 / n)
        for c in range(q2):
            sc_own[pl.ds(q2 * i + c, 1), :] = means[:, n * c:n * (c + 1)]
        return carry

    lax.fori_loop(0, own, score_row, 0)

    home_s = pltpu.make_async_copy(sc_own, o_sc.at[t, x], loc.at[1])
    home_s.start()
    s_out = []
    for d in (4, 3, 5, 2, 6, 7, 1):
        to = lax.rem(b + d, blks)
        s_out.append(remote(
            sc_own, o_sc.at[t, x], s_send.at[d], s_recv.at[b], (r, to)
        ))
        s_out[-1].start()

    for copy in ints + a_all + o_out + s_out:
        copy.wait_send()
    for cond, copy in m_out + relays + r_all:
        if cond is None:
            copy.wait_send()
        else:
            pl.when(cond)(copy.wait_send)
    home_o.wait()
    for d in range(1, blks):
        src = lax.rem(b + d, blks)
        sx, st = src // CORES, src % CORES
        remote(
            r_turn.at[:, pl.ds(0, width), :], o_res.at[st, pl.ds(rq * sx, rq)],
            o_send.at[d], o_recv.at[src], (r, b),
        ).wait_recv()
        remote(sc_own, o_sc.at[st, sx], s_send.at[d], s_recv.at[src], (r, b)).wait_recv()
    home_s.wait()


def on_device(rings, blks, acol, aval, mcol, mval, rpat, scol, cand):
    rows, per, n, _ = aval.shape
    slabs, _, qm = mcol.shape
    q2 = rpat.shape[2]
    chips = blks // CORES
    own = rows // chips
    window = 2 * rows + own
    dims = (rings, blks, rows, own, per, qm, q2, n)
    width = n // blks
    anywhere = pl.BlockSpec(memory_space=pl.ANY)
    dma = pltpu.SemaphoreType.DMA
    slots = blks * per
    res, sc = pl.pallas_call(
        functools.partial(kernel, dims),
        out_shape=(
            jax.ShapeDtypeStruct((slabs, rows * q2, width, n), jnp.bfloat16),
            jax.ShapeDtypeStruct((slabs, chips, own * q2, n), jnp.float32),
        ),
        in_specs=[anywhere] * 7,
        out_specs=(anywhere, anywhere),
        scratch_shapes=[
            pltpu.VMEM((blks, own, per, n, n), jnp.bfloat16),
            pltpu.VMEM((window * qm + 1, n, n), jnp.bfloat16),
            pltpu.VMEM((window * q2 + 1, n, n), jnp.bfloat16),
            pltpu.VMEM((own * q2, n, n), jnp.bfloat16),
            pltpu.VMEM((own * q2, n), jnp.float32),
            pltpu.VMEM((blks, per, rows), jnp.int32),
            pltpu.VMEM((3, qm, rows), jnp.int32),
            pltpu.VMEM((3, q2, rows), jnp.int32),
            pltpu.SMEM((blks, per, rows), jnp.int32),
            pltpu.SMEM((3, qm, rows), jnp.int32),
            pltpu.SMEM((3, q2, rows), jnp.int32),
            pltpu.SMEM(scol.shape, jnp.int32),
            pltpu.SMEM((slabs, q2, rows), jnp.int32),
            pltpu.SMEM((own * slots * q2,), jnp.int32),
            pltpu.SMEM((own * slots * q2,), jnp.int32),
            pltpu.SMEM((own * q2,), jnp.int32),
            dma((4 * chips,)), dma((2 * blks,)),
            dma((4 * chips,)), dma((4 * chips + 2,)),
            dma((11 * own,)), dma(((2 * chips + 1) * own,)),
            dma((blks,)), dma((blks,)), dma((3,)), dma((3,)), dma((3,)), dma((3,)),
            dma((blks,)), dma((blks,)), dma((blks,)), dma((blks,)),
            dma((6,)), dma((2,)), dma((7,)),
        ],
        compiler_params=pltpu.CompilerParams(
            collective_id=0, has_side_effects=True, vmem_limit_bytes=66 * 10**6
        ),
    )(
        scol, cand.swapaxes(1, 2), rpat.swapaxes(1, 2), acol.T, mcol.swapaxes(1, 2), aval,
        mval.reshape(slabs, rows * qm, n, n),
    )
    def finish(res_ref, sc_ref, o_ref, s_ref):
        b = lax.axis_index("blk")
        o_ref[...] = res_ref[...]
        for k in range(blks):

            @pl.when(b == k)
            def _():
                s_ref[...] = sc_ref[:, width * k:width * (k + 1)]

    res, sc = pl.pallas_call(
        finish,
        out_shape=(
            jax.ShapeDtypeStruct((slabs * rows * q2 * width, n), jnp.bfloat16),
            jax.ShapeDtypeStruct((slabs * rows * q2, width), jnp.float32),
        ),
    )(res.reshape(-1, n), sc.reshape(-1, n))
    resid = res.reshape(slabs, rows, q2, width, n).swapaxes(3, 4)
    return resid, sc.reshape(slabs, rows, q2, width)


def solution(mesh):
    placed = (
        P("rows", "blk"),
        P("rows", "blk", None, None),
        P(None, "rows", None),
        P(None, "rows", None, None, None),
        P(None, "rows", None),
        P(),
        P(None, "rows", None),
    )
    return jax.shard_map(
        functools.partial(on_device, mesh.shape["rows"], mesh.shape["blk"]),
        mesh=mesh,
        in_specs=placed,
        out_specs=(P(None, "rows", None, None, "blk"), P(None, "rows", None, "blk")),
        check_vma=False,
    )
```

```python
import functools

import jax
import jax.numpy as jnp
from jax import lax
from jax.experimental import pallas as pl
from jax.experimental.pallas import tpu as pltpu
from jax.sharding import PartitionSpec as P

MESH = pl.DeviceIdType.MESH
CORES = 2


def kernel(
    dims,
    scol_h, cand_h, rpat_h, acol_h, mcol_h, aval_h, mval_h,
    o_res, o_sc,
    a_win, m_win, r_win, r_turn, sc_own, ac_v, mc_v, rp_v,
    ac_s, mc_s, rp_s, scol_s, cand_s, idx_m, idx_r, diag,
    a_send, a_recv, m_send, m_recv, r_send, r_recv,
    ac_send, ac_recv, mc_send, mc_recv, rp_send, rp_recv,
    o_send, o_recv, s_send, s_recv, h_send, h_recv, loc,
):
    rings, blks, rows, own, per, qm, q2, n = dims
    chips = blks // CORES
    reach = rows
    total = rings * rows
    r, b = lax.axis_index("rows"), lax.axis_index("blk")
    x, t = b // CORES, b % CORES
    up, down = lax.rem(r + 1, rings), lax.rem(r + rings - 1, rings)
    mate = (r, CORES * x + (1 - t))
    mq, rq = own * qm, own * q2
    zero_m, zero_r = m_win.shape[0] - 1, r_win.shape[0] - 1

    def remote(src, dst, send, recv, where):
        return pltpu.make_async_remote_copy(
            src_ref=src, dst_ref=dst, send_sem=send, recv_sem=recv,
            device_id=where, device_id_type=MESH,
        )

    def across(d):
        return lax.rem(x + d, chips)

    def chip(d):
        return CORES * across(d) + t

    home_a = pltpu.make_async_copy(aval_h.at[pl.ds(own * x, own)], a_win.at[b], loc.at[0])
    home_m = pltpu.make_async_copy(
        mval_h.at[t], m_win.at[pl.ds(mq * (chips - x), mq * chips)], loc.at[1]
    )
    home_ac = pltpu.make_async_copy(acol_h, ac_v.at[b], loc.at[2])
    home_mc = pltpu.make_async_copy(mcol_h.at[t], mc_v.at[1], loc.at[3])
    home_rp = pltpu.make_async_copy(rpat_h.at[t], rp_v.at[1], loc.at[4])
    home_sc = pltpu.make_async_copy(scol_h, scol_s, loc.at[5])
    home_ca = pltpu.make_async_copy(cand_h, cand_s, loc.at[6])

    barrier = pltpu.get_barrier_semaphore()
    for ring in (up, down):
        pl.semaphore_signal(barrier, inc=1, device_id=(ring, b), device_id_type=MESH)
    for d in range(1, blks):
        pl.semaphore_signal(
            barrier, inc=1, device_id=(r, lax.rem(b + d, blks)), device_id_type=MESH
        )
    left, right = lax.rem(x + chips - 1, chips), lax.rem(x + 1, chips)
    for ring, side in ((up, left), (down, right)):
        pl.semaphore_signal(
            barrier, inc=1, device_id=(ring, CORES * side + t), device_id_type=MESH
        )
    for copy in (home_ac, home_mc, home_rp, home_sc, home_ca, home_a, home_m):
        copy.start()
    m_win[zero_m] = jnp.zeros((n, n), m_win.dtype)
    r_win[zero_r] = jnp.zeros((n, n), r_win.dtype)
    pl.semaphore_wait(barrier, blks - 1 + 4)

    hr = own // 2
    hops = (1, chips - 1) + tuple(range(2, chips - 1))
    a_all = []
    a_rows = ((0, own - 1), (own - 1, 1))

    def a_part(src, g):
        return a_win.at[src, pl.ds(*a_rows[g])]

    def a_copy(source, src, g, where):
        copy = remote(
            source, a_part(src, g), a_send.at[len(a_all)], a_recv.at[blks * g + src], where
        )
        copy.start()
        a_all.append(copy)

    def a_wait(src, g):
        remote(
            a_part(src, g), a_part(src, g), a_send.at[0], a_recv.at[blks * g + src], (r, b)
        ).wait_recv()

    ints = []
    for d in range(1, blks):
        to = lax.rem(b + d, blks)
        ints.append(remote(acol_h, ac_v.at[b], ac_send.at[d], ac_recv.at[b], (r, to)))
    for k, ring in ((0, up), (2, down)):
        ints.append(remote(mcol_h.at[t], mc_v.at[k], mc_send.at[k], mc_recv.at[k], (ring, b)))
        ints.append(remote(rpat_h.at[t], rp_v.at[k], rp_send.at[k], rp_recv.at[k], (ring, b)))
    for copy in ints:
        copy.start()


    def a_start(g):
        for d in hops:
            a_copy(aval_h.at[pl.ds(own * across(d) + a_rows[g][0], a_rows[g][1])], b, g, (r, chip(d)))

    last = chips - 1
    m_out = []
    mh = mq // 2
    for k in range(chips):
        for e in range(2):
            for cond, skip, j, h, slot, ring in (
                (x <= last - k, ((1, 0), (0, 0), (0, 1), (0, 2)), last - k, 1 - e, last - k - x, up),
                (x >= k, ((last - 1, 0), (last, 0), (last, 1), (last, 2)), k, e,
                 2 * chips + k - x, down),
            ):
                if k == 0 and e == 0:
                    cond &= (x != skip[0][0]) & (x != skip[1][0])
                elif k == 0 or (k == 1 and e == 0):
                    cond &= x != skip[1][0]
                safe = jnp.clip(slot, 0, 2 * chips)
                m_out.append((cond, remote(
                    mval_h.at[t, pl.ds(mq * j + mh * h, mh)],
                    m_win.at[pl.ds(mq * safe + mh * h, mh)],
                    m_send.at[len(m_out)], m_recv.at[2 * safe + h], (ring, b),
                )))
    for cond, copy in m_out:
        pl.when(cond)(copy.start)
    a_start(0)
    home_a.wait()
    a_copy(a_part(b, 0), b, 0, mate)
    for copy in (home_ac, home_mc, home_rp, home_sc, home_ca):
        copy.wait()
    for d in range(1, blks):
        src = lax.rem(b + d, blks)
        remote(acol_h, ac_v.at[src], ac_send.at[d], ac_recv.at[src], (r, b)).wait_recv()
    for k in (0, 2):
        remote(mcol_h.at[t], mc_v.at[k], mc_send.at[k], mc_recv.at[k], (r, b)).wait_recv()
        remote(rpat_h.at[t], rp_v.at[k], rp_send.at[k], rp_recv.at[k], (r, b)).wait_recv()
    moves = [
        pltpu.make_async_copy(ac_v, ac_s, loc.at[2]),
        pltpu.make_async_copy(mc_v, mc_s, loc.at[3]),
        pltpu.make_async_copy(rp_v, rp_s, loc.at[4]),
    ]
    for copy in moves:
        copy.start()
    for copy in moves:
        copy.wait()

    row0 = own * x
    slots = blks * per

    def table_row(i, carry):
        pats = [rp_s[1, p, row0 + i] for p in range(q2)]
        cands = [cand_s[t, c, row0 + i] for c in range(q2)]
        for p in range(q2):
            owner = scol_s[t, pats[p]]
            diag[q2 * i + p] = jnp.where(owner == rows * r + row0 + i, 1, 0)

        def table_slot(s, inner):
            col = ac_s[s // per, s % per, row0 + i]
            present = col >= 0
            w = lax.rem(col - rows * r + reach + total, total) - row0
            w = jnp.clip(w, 0, 2 * reach + own - 1)
            rel = w + row0
            side, line = lax.shift_right_logical(rel, rows.bit_length() - 1), rel & (rows - 1)
            mc = [mc_s[side, q, line] for q in range(qm)]
            rp = [rp_s[side, q, line] for q in range(q2)]
            for p in range(q2):
                at_m, at_r = jnp.int32(zero_m), jnp.int32(zero_r)
                for q in range(qm):
                    at_m = jnp.where(present & (mc[q] == pats[p]), w * qm + q, at_m)
                for q in range(q2):
                    at_r = jnp.where(present & (rp[q] == cands[p]), w * q2 + q, at_r)
                idx_m[(i * slots + s) * q2 + p] = at_m
                idx_r[(i * slots + s) * q2 + p] = at_r
            return inner

        return lax.fori_loop(0, slots, table_slot, carry)

    lax.fori_loop(0, own, table_row, 0)

    by_left, by_right = (r, CORES * left + t), (r, CORES * right + t)
    above, below = (up, b), (down, b)
    inner = (x >= 1) & (x <= last - 1)

    def m_rows(slot, first, count):
        return m_win.at[pl.ds(mq * slot + qm * first, qm * count)]

    def m_take(slot, h):
        part = m_rows(slot, hr * h, hr)
        remote(part, part, m_send.at[0], m_recv.at[2 * slot + h], (r, b)).wait_recv()

    relays = []
    for cond, needs, slots_of, rows_of, sem, where in (
        (x == last, ((0, 1), (0, 0)), (0, last), (1, own - 1), h_recv.at[1], by_right),
        (x == 0, ((2 * chips, 0), (2 * chips, 1)), (2 * chips, chips + 1), (0, own - 1),
         h_recv.at[1], by_left),
        (x == 1, ((2, 0),), (2, last), (0, 1), h_recv.at[0], by_left),
        (x == last - 1, ((2 * chips - 2, 1),), (2 * chips - 2, chips + 1), (own - 1, 1),
         h_recv.at[0], by_right),
        (inner, ((1, 1),), (1, 2), (hr, hr), m_recv.at[2 * 2 + 1], by_left),
        (inner, ((2 * chips - 1, 0),), (2 * chips - 1, 2 * chips - 2), (0, hr),
         m_recv.at[2 * (2 * chips - 2)], by_right),
    ):
        copy = remote(
            m_rows(slots_of[0], *rows_of), m_rows(slots_of[1], *rows_of),
            h_send.at[len(relays)], sem, where,
        )
        relays.append((cond, copy))

        def pass_on(needs=needs, copy=copy):
            for slot, h in needs:
                m_take(slot, h)
            copy.start()

        pl.when(cond)(pass_on)
    a_start(1)
    a_copy(a_part(b, 1), b, 1, mate)

    def a_swap(g):
        for d in hops:
            a_wait(chip(d), g)
            a_copy(a_part(chip(d), g), chip(d), g, mate)
        for d in range(chips):
            a_wait(CORES * across(d) + (1 - t), g)

    a_swap(0)
    home_m.wait()
    edge = (x == 0) | (x == last)
    for k in range(chips):
        for e in range(2):
            for cond, taken, slot, h in (
                (
                    k <= last - x,
                    ((x == last) & (k == 0)) | ((x == 1) & (k == 2) & (e == 1))
                    | (inner & (k == 1) & (e == 0)) | ((x == 0) & (k == last)),
                    k, 1 - e,
                ),
                (
                    k <= x,
                    ((x == 0) & (k == 0)) | ((x == last - 1) & (k == 2) & (e == 1))
                    | (inner & (k == 1) & (e == 0)) | ((x == last) & (k == last)),
                    2 * chips - k, e,
                ),
            ):
                pl.when(cond & jnp.logical_not(taken))(functools.partial(m_take, slot, h))

    def far_take(slot, one, rest):
        for k, span in ((0, (one, 1)), (1, (rest, own - 1))):
            part = m_rows(slot, *span)
            remote(part, part, h_send.at[0], h_recv.at[k], (r, b)).wait_recv()

    pl.when(x == 0)(lambda: far_take(last, 0, 1))
    pl.when(x == last)(lambda: far_take(chips + 1, own - 1, 0))

    def product(i, win, table):
        acc = None
        for k in range(blks):
            lhs = jnp.concatenate([a_win[k, i, s] for s in range(per)], axis=1)
            picks = []
            for s in range(per):
                at = (i * slots + k * per + s) * q2
                picks.append(jnp.concatenate([win[table[at + p]] for p in range(q2)], axis=1))
            rhs = jnp.concatenate(picks, axis=0)
            part = jnp.dot(lhs, rhs, preferred_element_type=jnp.float32)
            acc = part if acc is None else acc + part
        return acc

    eye = (
        lax.broadcasted_iota(jnp.int32, (n, n), 0) == lax.broadcasted_iota(jnp.int32, (n, n), 1)
    ).astype(jnp.float32)

    def resid_row(i, carry):
        summed = product(i, m_win, idx_m)
        for p in range(q2):
            block = summed[:, n * p:n * (p + 1)] - diag[q2 * i + p].astype(jnp.float32) * eye
            r_win[rq * chips + q2 * i + p] = block.astype(r_win.dtype)
        return carry

    pieces, direct = own, own - 1
    rh = rq // pieces
    r_all = []

    def piece(slot, h):
        return r_win.at[pl.ds(rq * slot + rh * h, rh)]

    def give(slot, h, to_slot, where, cond=None):
        if cond is not None:
            to_slot = jnp.clip(to_slot, 0, 2 * chips)
        copy = remote(
            piece(slot, h), piece(to_slot, h), r_send.at[len(r_all)],
            r_recv.at[pieces * to_slot + h], where,
        )
        r_all.append((cond, copy))
        if cond is None:
            copy.start()
        else:
            pl.when(cond)(copy.start)

    def take(slot, h, cond=None):
        def wait():
            remote(
                piece(slot, h), piece(slot, h), r_send.at[0], r_recv.at[pieces * slot + h], (r, b)
            ).wait_recv()

        if cond is None:
            wait()
        else:
            pl.when(cond)(wait)

    for h in range(pieces):
        if h == a_rows[1][0]:
            a_swap(1)
        resid_row(h, 0)
        give(chips, h, chips + x - right, by_right)
        give(chips, h, chips + x - left, by_left)
        give(chips, h, 0, above)
        give(chips, h, 2 * chips, below)

    for k in range(rq):
        block = r_win[rq * chips + k].astype(jnp.float32)
        r_turn[k] = block.T.astype(r_turn.dtype)

    at_left, at_right = chips + left - x, chips + right - x
    for h in range(pieces):
        take(at_left, h)
        if h < hr:
            give(at_left, h, chips + left - right, by_right)
        give(at_left, h, 2 * chips - 1, below, x >= 1)
        if h >= direct:
            give(at_left, h, 2 * chips - 2, (down, CORES * right + t), inner)
        take(at_right, h)
        if h >= hr:
            give(at_right, h, chips + right - left, by_left)
        give(at_right, h, 1, above, x <= last - 1)
        if h >= direct:
            give(at_right, h, 2, (up, CORES * left + t), inner)
        if h >= direct:
            give(at_left, h, last, above, x == 0)
            give(at_right, h, chips + 1, below, x == last)
        if h < direct:
            take(0, h, x == last)
            give(0, h, last, by_right, x == last)
            take(2 * chips, h, x == 0)
            give(2 * chips, h, chips + 1, by_left, x == 0)
    for h in range(pieces):
        take(1, h, x <= last - 1)
        if h < direct:
            give(1, h, 2, by_left, inner)
        take(2 * chips - 1, h, x >= 1)
        if h < direct:
            give(2 * chips - 1, h, 2 * chips - 2, by_right, inner)
    for h in range(pieces):
        take(0, h, None if h == direct else x != last)
        take(2 * chips, h, None if h == direct else x != 0)
        take(jnp.where(x < 2, chips + 2, chips - 2), h)
        take(2, h, x < 2)
        take(3, h, x == 0)
        take(2 * chips - 2, h, x >= 2)
        take(chips + 1, h, x == last)

    width = n // blks
    home_o = pltpu.make_async_copy(
        r_turn.at[:, pl.ds(width * b, width), :], o_res.at[t, pl.ds(rq * x, rq)], loc.at[0]
    )
    home_o.start()
    o_out = []
    for d in range(1, blks):
        to = lax.rem(b + d, blks)
        o_out.append(remote(
            r_turn.at[:, pl.ds(width * to, width), :], o_res.at[t, pl.ds(rq * x, rq)],
            o_send.at[d], o_recv.at[b], (r, to),
        ))
        o_out[-1].start()

    def score_row(i, carry):
        proj = product(i, r_win, idx_r)
        means = jnp.sum(proj * proj, axis=0, keepdims=True) * (1.0 / n)
        for c in range(q2):
            sc_own[pl.ds(q2 * i + c, 1), :] = means[:, n * c:n * (c + 1)]
        return carry

    lax.fori_loop(0, own, score_row, 0)

    home_s = pltpu.make_async_copy(sc_own, o_sc.at[t, x], loc.at[1])
    home_s.start()
    s_out = []
    for d in (4, 3, 5, 2, 6, 7, 1):
        to = lax.rem(b + d, blks)
        s_out.append(remote(
            sc_own, o_sc.at[t, x], s_send.at[d], s_recv.at[b], (r, to)
        ))
        s_out[-1].start()

    for copy in ints + a_all + o_out + s_out:
        copy.wait_send()
    for cond, copy in m_out + relays + r_all:
        if cond is None:
            copy.wait_send()
        else:
            pl.when(cond)(copy.wait_send)
    home_o.wait()
    for d in range(1, blks):
        src = lax.rem(b + d, blks)
        sx, st = src // CORES, src % CORES
        remote(
            r_turn.at[:, pl.ds(0, width), :], o_res.at[st, pl.ds(rq * sx, rq)],
            o_send.at[d], o_recv.at[src], (r, b),
        ).wait_recv()
        remote(sc_own, o_sc.at[st, sx], s_send.at[d], s_recv.at[src], (r, b)).wait_recv()
    home_s.wait()


def on_device(rings, blks, acol, aval, mcol, mval, rpat, scol, cand):
    rows, per, n, _ = aval.shape
    slabs, _, qm = mcol.shape
    q2 = rpat.shape[2]
    chips = blks // CORES
    own = rows // chips
    window = 2 * rows + own
    dims = (rings, blks, rows, own, per, qm, q2, n)
    width = n // blks
    anywhere = pl.BlockSpec(memory_space=pl.ANY)
    dma = pltpu.SemaphoreType.DMA
    slots = blks * per
    res, sc = pl.pallas_call(
        functools.partial(kernel, dims),
        out_shape=(
            jax.ShapeDtypeStruct((slabs, rows * q2, width, n), jnp.bfloat16),
            jax.ShapeDtypeStruct((slabs, chips, own * q2, n), jnp.float32),
        ),
        in_specs=[anywhere] * 7,
        out_specs=(anywhere, anywhere),
        scratch_shapes=[
            pltpu.VMEM((blks, own, per, n, n), jnp.bfloat16),
            pltpu.VMEM((window * qm + 1, n, n), jnp.bfloat16),
            pltpu.VMEM((window * q2 + 1, n, n), jnp.bfloat16),
            pltpu.VMEM((own * q2, n, n), jnp.bfloat16),
            pltpu.VMEM((own * q2, n), jnp.float32),
            pltpu.VMEM((blks, per, rows), jnp.int32),
            pltpu.VMEM((3, qm, rows), jnp.int32),
            pltpu.VMEM((3, q2, rows), jnp.int32),
            pltpu.SMEM((blks, per, rows), jnp.int32),
            pltpu.SMEM((3, qm, rows), jnp.int32),
            pltpu.SMEM((3, q2, rows), jnp.int32),
            pltpu.SMEM(scol.shape, jnp.int32),
            pltpu.SMEM((slabs, q2, rows), jnp.int32),
            pltpu.SMEM((own * slots * q2,), jnp.int32),
            pltpu.SMEM((own * slots * q2,), jnp.int32),
            pltpu.SMEM((own * q2,), jnp.int32),
            dma((4 * chips,)), dma((2 * blks,)),
            dma((4 * chips,)), dma((4 * chips + 2,)),
            dma((11 * own,)), dma(((2 * chips + 1) * own,)),
            dma((blks,)), dma((blks,)), dma((3,)), dma((3,)), dma((3,)), dma((3,)),
            dma((blks,)), dma((blks,)), dma((blks,)), dma((blks,)),
            dma((6,)), dma((2,)), dma((7,)),
        ],
        compiler_params=pltpu.CompilerParams(
            collective_id=0, has_side_effects=True, vmem_limit_bytes=66 * 10**6
        ),
    )(
        scol, cand.swapaxes(1, 2), rpat.swapaxes(1, 2), acol.T, mcol.swapaxes(1, 2), aval,
        mval.reshape(slabs, rows * qm, n, n),
    )
    def finish(res_ref, sc_ref, o_ref, s_ref):
        b = lax.axis_index("blk")
        o_ref[...] = res_ref[...]
        for k in range(blks):

            @pl.when(b == k)
            def _():
                s_ref[...] = sc_ref[:, width * k:width * (k + 1)]

    res, sc = pl.pallas_call(
        finish,
        out_shape=(
            jax.ShapeDtypeStruct((slabs * rows * q2 * width, n), jnp.bfloat16),
            jax.ShapeDtypeStruct((slabs * rows * q2, width), jnp.float32),
        ),
    )(res.reshape(-1, n), sc.reshape(-1, n))
    resid = res.reshape(slabs, rows, q2, width, n).swapaxes(3, 4)
    return resid, sc.reshape(slabs, rows, q2, width)


def solution(mesh):
    placed = (
        P("rows", "blk"),
        P("rows", "blk", None, None),
        P(None, "rows", None),
        P(None, "rows", None, None, None),
        P(None, "rows", None),
        P(),
        P(None, "rows", None),
    )
    return jax.shard_map(
        functools.partial(on_device, mesh.shape["rows"], mesh.shape["blk"]),
        mesh=mesh,
        in_specs=placed,
        out_specs=(P(None, "rows", None, None, "blk"), P(None, "rows", None, "blk")),
        check_vma=False,
    )
```
